256 devices in a mesh: src: 8 (over z_lo, core), tgt: 32 (over y, x, z_hi).
Axes of the slice: x: 4, y: 4, z: 8 (z_hi: 2, z_lo: 4; z = z_hi * 4 + z_lo), core: 2. Of those that a mesh axis runs over, the one named last changes fastest.
Arguments:
- src_feat: bfloat16 [16, 128, 1024], P('src', None, 'tgt'), may hold values from -6 to 6
- tgt_feat: bfloat16 [128, 96, 1024], P('tgt'), may hold values from -6 to 6
- w_src: bfloat16 [8, 3, 3], replicated, may hold values from -2 to 2
- b_src: float32 [8], replicated, may hold values from -3 to 3
- w_tgt: bfloat16 [8, 8, 3, 3], replicated, may hold values from -0.75 to 0.75
- b_tgt: float32 [8], replicated, may hold values from -3 to 3
- w_out: float32 [8], replicated, may hold values from -2 to 2
- cotangent: bfloat16 [128, 96, 16, 128], P('tgt', None, 'src'), may hold values from -6 to 6
Outputs:
- score: bfloat16 [128, 96, 16, 128], P('tgt', None, 'src')
- grad_src: float32 [1024, 16, 128], P('tgt', 'src')
- grad_tgt: float32 [128, 96, 1024], P('tgt', None, 'src')
The draws below stay inside these ranges and needn't reach their ends.
All inputs are finite; a program needn't handle non-finite values.
Results may differ from the reference program's by a relative error of at most 0.0064.
Values may be sent and summed in bfloat16 or wider, within the bound.
No kernel may reach another device: no remote copies, remote signals or barrier semaphores. Data moves between devices by JAX's collectives and lax.ppermute only.
A program may use at most 128 MiB of HBM per device.

```python
import jax
import jax.numpy as jnp
from jax import lax

C = 1024
CH = 8
SW = 128
TR = 4
TW = 96
BAND = 16
TROWS = 128


def level_of(stream_key, dims, pieces, smallest, high):
    loudness, own = 1.0, jax.random.fold_in(stream_key, 6)
    for position, blocks in pieces:
        steps = jnp.exp(jax.random.uniform(jax.random.fold_in(own, position), (blocks,), jnp.float32, smallest / len(pieces), high / len(pieces)))
        loudness = loudness * jnp.repeat(steps, dims[position] // blocks).reshape([-1 if axis == position else 1 for axis in range(len(dims))])
    return loudness


def centred(key, dims, scale, limit, shards=(), kind=jnp.bfloat16):
    result = scale * jax.random.normal(key, dims, jnp.float32)
    if shards:
        result = result * level_of(key, dims, shards, -0.22, 0.18)
    return jnp.clip(result, -limit, limit).astype(kind)


def setup_inputs(seed: int = 0) -> dict:
    seeds = jax.random.split(jax.random.key(seed), 9)
    src_feat = centred(seeds[0], (BAND, SW, C), 1.0, 6.0, ((0, 8), (2, 32)))
    tgt_feat = centred(seeds[1], (TROWS, TW, C), 1.0, 6.0, ((0, 32),))
    w_src = centred(seeds[2], (CH, 3, 3), 9 ** -0.5, 2.0)
    b_src = centred(seeds[3], (CH,), 0.5, 3.0, (), jnp.float32)
    w_tgt = centred(seeds[4], (CH, CH, 3, 3), (9 * CH) ** -0.5, 0.75)
    b_tgt = centred(seeds[5], (CH,), 0.5, 3.0, (), jnp.float32)
    w_out = centred(seeds[6], (CH,), CH ** -0.5, 2.0, (), jnp.float32)
    cotangent = centred(seeds[7], (TROWS, TW, BAND, SW), 1.0, 6.0, ((0, 32), (2, 8)))
    return dict(src_feat=src_feat, tgt_feat=tgt_feat, w_src=w_src, b_src=b_src, w_tgt=w_tgt, b_tgt=b_tgt, w_out=w_out, cotangent=cotangent)


def src_conv(corr, w_src, b_src):
    padded = jnp.pad(corr.astype(jnp.float32), ((0, 0), (0, 0), (1, 1), (1, 1)))
    rows_i = corr.shape[2]
    cols_j = corr.shape[3]
    total = jnp.zeros((w_src.shape[0],) + corr.shape, jnp.float32) + b_src[:, None, None, None, None]
    for a in range(3):
        for b in range(3):
            weight = w_src[:, a, b].astype(jnp.float32)[:, None, None, None, None]
            total = total + weight * padded[None, :, :, a:a + rows_i, b:b + cols_j]
    return total


def tgt_conv(hidden, w_tgt, b_tgt):
    padded = jnp.pad(hidden.astype(jnp.float32), ((0, 0), (0, 0), (1, 1), (0, 0), (0, 0)))
    rows_k = hidden.shape[1] - 2
    cols_l = hidden.shape[2]
    total = jnp.zeros((w_tgt.shape[0], rows_k) + hidden.shape[2:], jnp.float32) + b_tgt[:, None, None, None, None]
    for a in range(3):
        for b in range(3):
            total = total + jnp.einsum('op,pklij->oklij', w_tgt[:, :, a, b].astype(jnp.float32), padded[:, a:a + rows_k, b:b + cols_l])
    return total


def tgt_transpose(grads, w_tgt):
    padded = jnp.pad(grads.astype(jnp.float32), ((0, 0), (0, 0), (1, 1), (0, 0), (0, 0)))
    rows_k = grads.shape[1] - 2
    cols_l = grads.shape[2]
    total = jnp.zeros((w_tgt.shape[1], rows_k) + grads.shape[2:], jnp.float32)
    for a in range(3):
        for b in range(3):
            total = total + jnp.einsum('op,oklij->pklij', w_tgt[:, :, a, b].astype(jnp.float32), padded[:, 2 - a:2 - a + rows_k, 2 - b:2 - b + cols_l])
    return total


def src_transpose(grads, w_src):
    padded = jnp.pad(grads.astype(jnp.float32), ((0, 0), (0, 0), (0, 0), (0, 0), (1, 1)))
    rows_i = grads.shape[3] - 2
    cols_j = grads.shape[4]
    total = jnp.zeros(grads.shape[1:3] + (rows_i, cols_j), jnp.float32)
    for a in range(3):
        for b in range(3):
            total = total + jnp.einsum('o,oklij->klij', w_src[:, a, b].astype(jnp.float32), padded[:, :, :, 2 - a:2 - a + rows_i, 2 - b:2 - b + cols_j])
    return total


def reference(src_feat, tgt_feat, w_src, b_src, w_tgt, b_tgt, w_out, cotangent):
    scale = C ** -0.5
    src_flat = src_feat.reshape(BAND * SW, C)
    tgt_pad = jnp.pad(tgt_feat, ((2, 2), (0, 0), (0, 0)))
    cot_pad = jnp.pad(cotangent.astype(jnp.float32), ((1, 1), (0, 0), (0, 0), (0, 0)))
    gains = w_out[:, None, None, None, None]

    def block(carry, blk):
        start = (blk * TR).astype(jnp.int32)
        rows = lax.dynamic_slice_in_dim(tgt_pad, start, TR + 4, 0)
        flat = rows.reshape((TR + 4) * TW, C)
        raw = jnp.dot(flat, src_flat.T, preferred_element_type=jnp.float32)
        corr = (raw * scale).astype(jnp.bfloat16).reshape(TR + 4, TW, BAND, SW)
        hidden = src_conv(corr, w_src, b_src)
        global_rows = start - 2 + jnp.arange(TR + 4, dtype=jnp.int32)
        valid = (global_rows >= 0) & (global_rows < TROWS)
        hidden = jnp.where(valid[None, :, None, None, None], hidden, 0.0).astype(jnp.bfloat16)
        pre = tgt_conv(hidden, w_tgt, b_tgt)
        score_blk = jnp.sum(gains * jax.nn.silu(pre[:, 1:TR + 1]), axis=0).astype(jnp.bfloat16)
        cot = lax.dynamic_slice_in_dim(cot_pad, start, TR + 2, 0)
        sig = jax.nn.sigmoid(pre)
        g_pre = (cot[None] * gains * (sig * (1.0 + pre * (1.0 - sig)))).astype(jnp.bfloat16)
        g_hidden = tgt_transpose(g_pre, w_tgt).astype(jnp.bfloat16)
        g_hidden = jnp.pad(g_hidden, ((0, 0), (0, 0), (0, 0), (1, 1), (0, 0)))
        g_corr = src_transpose(g_hidden, w_src).astype(jnp.bfloat16)
        g_flat = g_corr.reshape(TR * TW, BAND * SW)
        own = rows[2:2 + TR].reshape(TR * TW, C)
        g_src = lax.dot_general(own, g_flat, (((0,), (0,)), ((), ())), preferred_element_type=jnp.float32) * scale
        g_tgt = (jnp.dot(g_flat, src_flat, preferred_element_type=jnp.float32) * scale).reshape(TR, TW, C)
        return carry + g_src, (score_blk, g_tgt)

    init = jnp.zeros((C, BAND * SW), jnp.float32)
    total, (scores, g_tgts) = lax.scan(block, init, jnp.arange(TROWS // TR, dtype=jnp.int32))
    score = scores.reshape(TROWS, TW, BAND, SW)
    grad_tgt = g_tgts.reshape(TROWS, TW, C)
    grad_src = total.reshape(C, BAND, SW)
    return score, grad_src, grad_tgt
```

```python
import functools

import jax
import jax.numpy as jnp
import numpy as np
from jax import lax
from jax.experimental import pallas as pl
from jax.experimental.pallas import tpu as pltpu
from jax.sharding import PartitionSpec as P

BF = jnp.bfloat16
F32 = jnp.float32
TAPS = 10


def shift_lanes(v, by):
    n = v.shape[1]
    lane = lax.broadcasted_iota(jnp.int32, v.shape, 1)
    edge = 0 if by == 1 else n - 1
    return jnp.where(lane == edge, 0.0, pltpu.roll(v, by % n, 1))


def conv_kernel(
    cols,
    wf_ref, wb_ref, bias_ref, wout_ref,
    own_ref, up_ref, dn_ref, lo_ref, hi_ref, cot_ref, cup_ref, cdn_ref,
    score_ref, g_ref, glo_ref, ghi_ref,
    cs, rows, cotf, cots, gp, sc, gs,
):
    for k in range(8):
        ref, at = (up_ref, k) if k < 2 else (own_ref, k - 2) if k < 6 else (dn_ref, k - 6)
        plane = ref[at].astype(F32)
        cs[0, pl.ds(k, cols, stride=8), :] = lo_ref[k].astype(F32)
        cs[1, pl.ds(k, cols, stride=8), :] = plane[:, :128]
        cs[2, pl.ds(k, cols, stride=8), :] = plane[:, 128:]
        cs[3, pl.ds(k, cols, stride=8), :] = hi_ref[k].astype(F32)
    zeros = jnp.zeros((cols, 128), F32)
    cotf[pl.ds(0, 2 * cols), :] = cup_ref[...].astype(F32)
    cotf[pl.ds(2 * cols, 8 * cols), :] = cot_ref[...].astype(F32)
    cotf[pl.ds(10 * cols, 2 * cols), :] = cdn_ref[...].astype(F32)
    for i in range(2):
        cots[i, pl.ds(0, cols, stride=8), :] = zeros
        cots[i, pl.ds(7, cols, stride=8), :] = zeros
        for k in range(6):
            cots[i, pl.ds(k + 1, cols, stride=8), :] = cotf[pl.ds(2 * cols * k + i, cols, stride=2), :]

    group = TAPS * 8
    for end in (0, cols + 1):
        rows[pl.ds(end * group, group), :] = jnp.zeros((group, 256), BF)
        gp[pl.ds(end * 64, 64), :] = jnp.zeros((64, 256), BF)

    def spread(l, _):
        at = pl.multiple_of(l * 8, 8)
        taps = []
        for i in range(4):
            v = cs[i, pl.ds(at, 8), :]
            taps.append((shift_lanes(v, 1), v, shift_lanes(v, -1)))
        for i in range(2):
            block = [taps[i + a][b] for a in range(3) for b in range(3)]
            block.append(jnp.zeros((8, 128), F32))
            rows[pl.ds(pl.multiple_of((l + 1) * group, 16), group), pl.ds(i * 128, 128)] = jnp.concatenate(block, 0).astype(BF)
        return 0

    lax.fori_loop(0, cols, spread, 0, unroll=4)

    wf = wf_ref[...]
    wb = wb_ref[...]

    def forward(l, _):
        kind = jnp.where(l == 0, 0, jnp.where(l == cols - 1, 2, 1))
        window = rows[pl.ds(pl.multiple_of(l * group, 16), 3 * group), :]
        u = jnp.dot(wf, window, preferred_element_type=F32)
        u = u + bias_ref[pl.ds(pl.multiple_of(kind * 64, 64), 64), :]
        th = jnp.tanh(u)
        q = u * th
        g = (1.0 + u) + th * (1.0 - q)
        s = u + q
        at = pl.multiple_of(l * 8, 8)
        cot = jnp.concatenate([cots[0, pl.ds(at, 8), :], cots[1, pl.ds(at, 8), :]], 1)
        total = jnp.zeros((8, 256), F32)
        out = []
        for o in range(8):
            w = wout_ref[o]
            total = total + w * s[o * 8:o * 8 + 8]
            out.append(g[o * 8:o * 8 + 8] * (cot * (0.5 * w)))
        gp[pl.ds(pl.multiple_of((l + 1) * 64, 64), 64), :] = jnp.concatenate(out, 0).astype(BF)
        sc[0, pl.ds(at, 8), :] = total[:, :128]
        sc[1, pl.ds(at, 8), :] = total[:, 128:]
        return 0

    lax.fori_loop(0, cols, forward, 0, unroll=4)

    def backward(m, _):
        window = gp[pl.ds(pl.multiple_of(m * 128, 128), 256), :]
        t = jnp.dot(wb, window, preferred_element_type=F32)
        at = pl.multiple_of(m * 8, 8)
        for io in range(4):
            part = []
            for b in range(3):
                pieces = []
                for a in range(3):
                    i = io - a
                    if 0 <= i < 2:
                        pieces.append(t[(b * 3 + a) * 8:(b * 3 + a) * 8 + 8, i * 128:(i + 1) * 128])
                part.append(functools.reduce(jnp.add, pieces))
            gs[io, pl.ds(at, 8), :] = shift_lanes(part[0], -1) + part[1] + shift_lanes(part[2], 1)
        return 0

    lax.fori_loop(0, cols // 2, backward, 0, unroll=4)

    for k in range(4):
        for i in range(2):
            cotf[pl.ds(2 * cols * k + i, cols, stride=2), :] = sc[i, pl.ds(k + 2, cols, stride=8), :]
    score_ref[...] = cotf[pl.ds(0, 8 * cols), :].astype(BF)
    for k in range(4):
        here = pl.ds(k * cols, cols)
        glo_ref[here, :] = gs[0, pl.ds(k, cols, stride=4), :].astype(BF)
        g_ref[here, pl.ds(0, 128)] = gs[1, pl.ds(k, cols, stride=4), :]
        g_ref[here, pl.ds(128, 128)] = gs[2, pl.ds(k, cols, stride=4), :]
        ghi_ref[here, :] = gs[3, pl.ds(k, cols, stride=4), :].astype(BF)


def conv(cols, weights, own, up, dn, lo, hi, cot, cup, cdn):
    wf, wb, bias, w_out = weights
    vmem = pl.BlockSpec(memory_space=pltpu.VMEM)
    smem = pl.BlockSpec(memory_space=pltpu.SMEM)
    n = 4 * cols
    return pl.pallas_call(
        functools.partial(conv_kernel, cols),
        out_shape=(
            jax.ShapeDtypeStruct((8 * cols, 128), BF),
            jax.ShapeDtypeStruct((n, 256), F32),
            jax.ShapeDtypeStruct((n, 128), BF),
            jax.ShapeDtypeStruct((n, 128), BF),
        ),
        in_specs=[vmem, vmem, vmem, smem] + [vmem] * 8,
        out_specs=(vmem,) * 4,
        scratch_shapes=[
            pltpu.VMEM((4, 8 * cols, 128), F32),
            pltpu.VMEM(((cols + 2) * TAPS * 8, 256), BF),
            pltpu.VMEM((12 * cols, 128), F32),
            pltpu.VMEM((2, 8 * cols, 128), F32),
            pltpu.VMEM(((cols + 2) * 64, 256), BF),
            pltpu.VMEM((2, 8 * cols, 128), F32),
            pltpu.VMEM((4, 4 * cols, 128), F32),
        ],
        compiler_params=pltpu.CompilerParams(vmem_limit_bytes=40 * 2**20),
        cost_estimate=pl.CostEstimate(flops=4 * 10**9, transcendentals=10**7, bytes_accessed=4 * 10**6),
    )(wf, wb, bias, w_out, own, up, dn, lo, hi, cot, cup, cdn)


def filters(w_src, b_src, w_tgt, b_tgt, first_row, total_rows):
    both = jnp.einsum(
        "opde,pab->odeab", w_tgt.astype(F32), w_src.astype(F32), precision=lax.Precision.HIGHEST
    )
    up = np.zeros((3, 8, 8), np.float32)
    for d in range(3):
        for m in range(1, 7):
            up[d, m, m + d - 1] = 1
    flat = jnp.pad(both.reshape(8, 3, 3, 9), ((0, 0), (0, 0), (0, 0), (0, TAPS - 9)))
    wf = (0.5 * jnp.einsum("odex,dmk->omexk", flat, up)).reshape(64, 3 * TAPS * 8).astype(BF)
    back = np.zeros((3, 4, 8), np.float32)
    side = np.zeros((3, 2, 4), np.float32)
    for d in range(3):
        for k in range(4):
            back[d, k, k + 3 - d] = 1
        for s in range(2):
            side[d, s, s + 2 - d] = 1
    spots = np.einsum("dkm,esl->desklm", back, side)
    wb = jnp.einsum("odeab,desklm->baskyom".replace("y", "l"), both, spots).reshape(72, 256).astype(BF)
    lift = jnp.einsum(
        "opde,p->ode", w_tgt.astype(F32), b_src, precision=lax.Precision.HIGHEST
    )
    row = first_row - 2 + jnp.arange(8)
    inside = ((row >= 0) & (row < total_rows)).astype(F32)
    edge = np.ones((3, 3), np.float32)
    edge[0, 0] = 0
    edge[2, 2] = 0
    along = jnp.einsum("ode,te->tod", lift, edge, precision=lax.Precision.HIGHEST)
    reach = jnp.einsum("dmk,k->md", up, inside, precision=lax.Precision.HIGHEST)
    bias = b_tgt[None, :, None] + jnp.einsum("tod,md->tom", along, reach, precision=lax.Precision.HIGHEST)
    bias = jnp.broadcast_to((0.5 * bias).reshape(192, 1), (192, 256))
    return wf, wb, bias


def permuted(x, pairs):
    return lax.ppermute(x, ("src", "tgt"), pairs)


def body(src_feat, tgt_feat, w_src, b_src, w_tgt, b_tgt, w_out, cotangent):
    rows_k, cols, rows_i, cols_j = cotangent.shape
    chans = tgt_feat.shape[2]
    scale = chans ** (-0.5)
    n_src, n_tgt = lax.axis_size("src"), lax.axis_size("tgt")
    s, t = lax.axis_index("src"), lax.axis_index("tgt")
    block = chans // n_tgt

    def joint(move):
        out = []
        for a in range(n_src):
            for b in range(n_tgt):
                c, d = move(a, b)
                if 0 <= c < n_src and 0 <= d < n_tgt:
                    out.append((a * n_tgt + b, c * n_tgt + d))
        return out

    tgt_up = joint(lambda a, b: (a, b + 1))
    tgt_dn = joint(lambda a, b: (a, b - 1))
    src_up = joint(lambda a, b: (a + 1, b))
    src_dn = joint(lambda a, b: (a - 1, b))

    weights = filters(w_src, b_src, w_tgt, b_tgt, t * rows_k, rows_k * n_tgt)
    tgt_flat = tgt_feat.reshape(rows_k * cols, chans)

    piece = src_feat.reshape(rows_i * cols_j, block).T
    src_t = lax.all_to_all(
        jnp.broadcast_to(piece[None], (n_tgt, block, rows_i * cols_j)), "tgt", 0, 0, tiled=True
    ).reshape(chans, rows_i * cols_j)

    raw = jnp.dot(tgt_flat, src_t, preferred_element_type=F32)
    own = (raw * scale).astype(BF).reshape(rows_k, cols, rows_i * cols_j)
    cot = cotangent.reshape(rows_k, cols * rows_i, cols_j)
    up = permuted(own[rows_k - 2:], tgt_up)
    dn = permuted(own[:2], tgt_dn)
    cup = permuted(cot[rows_k - 1], tgt_up)
    cdn = permuted(cot[0], tgt_dn)
    tall = jnp.concatenate([up, own, dn], 0)
    lo = permuted(tall[:, :, cols_j:], src_up)
    hi = permuted(tall[:, :, :cols_j], src_dn)

    score, g_own, g_lo, g_hi = conv(
        cols, (*weights, w_out), own, up, dn, lo, hi,
        cot.reshape(rows_k * cols * rows_i, cols_j), cup, cdn,
    )
    from_hi = permuted(g_lo, src_dn)
    from_lo = permuted(g_hi, src_up)
    g = (g_own + jnp.concatenate([from_lo, from_hi], 1).astype(F32)).astype(BF)

    part = lax.dot_general(tgt_flat, g, (((0,), (0,)), ((), ())), preferred_element_type=F32) * scale
    parts = lax.all_to_all(
        part.astype(BF).reshape(n_tgt, block, rows_i * cols_j), "tgt", 0, 0, tiled=True
    )
    grad_src = jnp.sum(parts.astype(F32), 0).reshape(block, rows_i, cols_j)

    z, core = s // 2, s % 2
    cut = src_t.reshape(n_src, chans // n_src, rows_i * cols_j)
    hops = n_src // 2

    def blocks(side):
        return jnp.concatenate([lax.dynamic_index_in_dim(cut, (z ^ m) * 2 + side, 0, False) for m in range(hops)], 0)

    over = (((1,), (1,)), ((), ()))
    mine = lax.dot_general(g, blocks(core), over, preferred_element_type=F32) * scale
    other = lax.dot_general(g, blocks(1 - core), over, preferred_element_type=F32) * scale
    got = permuted(other.astype(BF), joint(lambda a, b: (a ^ 1, b)))
    both = mine + got.astype(F32)
    width = chans // n_src
    total = both[:, :width]
    for m in range(1, hops):
        total = total + permuted(
            both[:, m * width:(m + 1) * width].astype(BF), joint(lambda a, b, m=m: (a ^ (2 * m), b))
        ).astype(F32)
    grad_tgt = total.reshape(rows_k, cols, width)
    return (score.reshape(cotangent.shape), grad_src, grad_tgt)


def solution(mesh):
    placed = (
        P("src", None, "tgt"),
        P("tgt", None, None),
        P(),
        P(),
        P(),
        P(),
        P(),
        P("tgt", None, "src", None),
    )
    return jax.shard_map(
        body,
        mesh=mesh,
        in_specs=placed,
        out_specs=(P("tgt", None, "src", None), P("tgt", "src", None), P("tgt", None, "src")),
        check_vma=False,
    )
```

```python
import functools

import jax
import jax.numpy as jnp
import numpy as np
from jax import lax
from jax.experimental import pallas as pl
from jax.experimental.pallas import tpu as pltpu
from jax.sharding import PartitionSpec as P

BF = jnp.bfloat16
F32 = jnp.float32
TAPS = 10


def shift_lanes(v, by):
    n = v.shape[1]
    lane = lax.broadcasted_iota(jnp.int32, v.shape, 1)
    edge = 0 if by == 1 else n - 1
    return jnp.where(lane == edge, 0.0, pltpu.roll(v, by % n, 1))


def conv_kernel(
    cols,
    core_ref, wout_ref, wf_ref, wb_ref, bias_ref,
    own_ref, up_ref, dn_ref, far_ref, near_ref, cot_ref,
    score_ref, g_ref, far_out, near_out,
    cs, rows, cotf, cots, gp, sc, gs,
):
    first = core_ref[0] == 0

    for k in range(8):
        if 2 <= k < 6:
            left = own_ref[pl.ds((k - 2) * cols, cols), pl.ds(0, 128)]
            right = own_ref[pl.ds((k - 2) * cols, cols), pl.ds(128, 128)]
        else:
            ref, at = (up_ref, k) if k < 2 else (dn_ref, k - 6)
            left = ref[pl.ds(at * cols, cols), :]
            right = ref[pl.ds((at + 2) * cols, cols), :]
        here = pl.ds(k * cols, cols)
        far, near = far_ref[here, :].astype(F32), near_ref[here, :].astype(F32)
        where = pl.ds(k, cols, stride=8)
        cs[0, where, :] = jnp.where(first, far, near)
        cs[1, where, :] = left.astype(F32)
        cs[2, where, :] = right.astype(F32)
        cs[3, where, :] = jnp.where(first, near, far)
    zeros = jnp.zeros((cols, 128), F32)
    cotf[pl.ds(0, 2 * cols), :] = up_ref[pl.ds(4 * cols, 2 * cols), :].astype(F32)
    cotf[pl.ds(2 * cols, 8 * cols), :] = cot_ref[...].astype(F32)
    cotf[pl.ds(10 * cols, 2 * cols), :] = dn_ref[pl.ds(4 * cols, 2 * cols), :].astype(F32)
    for i in range(2):
        cots[i, pl.ds(0, cols, stride=8), :] = zeros
        cots[i, pl.ds(7, cols, stride=8), :] = zeros
        for k in range(6):
            cots[i, pl.ds(k + 1, cols, stride=8), :] = cotf[pl.ds(2 * cols * k + i, cols, stride=2), :]

    group = TAPS * 8
    for end in (0, cols + 1):
        rows[pl.ds(end * group, group), :] = jnp.zeros((group, 256), BF)
        gp[pl.ds(end * 64, 64), :] = jnp.zeros((64, 256), BF)

    def spread(l, _):
        at = pl.multiple_of(l * 8, 8)
        taps = []
        for i in range(4):
            v = cs[i, pl.ds(at, 8), :]
            taps.append((shift_lanes(v, 1), v, shift_lanes(v, -1)))
        for i in range(2):
            block = [taps[i + a][b] for a in range(3) for b in range(3)]
            block.append(jnp.zeros((8, 128), F32))
            rows[pl.ds(pl.multiple_of((l + 1) * group, 16), group), pl.ds(i * 128, 128)] = jnp.concatenate(block, 0).astype(BF)
        return 0

    lax.fori_loop(0, cols, spread, 0, unroll=16)

    wf = wf_ref[...]
    wb = wb_ref[...]

    def forward(l, _):
        kind = jnp.where(l == 0, 0, jnp.where(l == cols - 1, 2, 1))
        window = rows[pl.ds(pl.multiple_of(l * group, 16), 3 * group), :]
        u = jnp.dot(wf, window, preferred_element_type=F32)
        u = u + bias_ref[pl.ds(pl.multiple_of(kind * 64, 64), 64), :]
        th = jnp.tanh(u)
        q = u * th
        g = (1.0 + u) + th * (1.0 - q)
        s = u + q
        at = pl.multiple_of(l * 8, 8)
        cot = jnp.concatenate([cots[0, pl.ds(at, 8), :], cots[1, pl.ds(at, 8), :]], 1)
        total = jnp.zeros((8, 256), F32)
        out = []
        for o in range(8):
            w = wout_ref[o]
            total = total + w * s[o * 8:o * 8 + 8]
            out.append(g[o * 8:o * 8 + 8] * (cot * (0.5 * w)))
        gp[pl.ds(pl.multiple_of((l + 1) * 64, 64), 64), :] = jnp.concatenate(out, 0).astype(BF)
        sc[0, pl.ds(at, 8), :] = total[:, :128]
        sc[1, pl.ds(at, 8), :] = total[:, 128:]
        return 0

    lax.fori_loop(0, cols, forward, 0, unroll=32)

    def backward(m, _):
        window = gp[pl.ds(pl.multiple_of(m * 128, 128), 256), :]
        t = jnp.dot(wb, window, preferred_element_type=F32)
        at = pl.multiple_of(m * 8, 8)
        for io in range(4):
            part = []
            for b in range(3):
                pieces = []
                for a in range(3):
                    i = io - a
                    if 0 <= i < 2:
                        pieces.append(t[(b * 3 + a) * 8:(b * 3 + a) * 8 + 8, i * 128:(i + 1) * 128])
                part.append(functools.reduce(jnp.add, pieces))
            gs[io, pl.ds(at, 8), :] = shift_lanes(part[0], -1) + part[1] + shift_lanes(part[2], 1)
        return 0

    lax.fori_loop(0, cols // 2, backward, 0, unroll=16)

    for k in range(4):
        for i in range(2):
            cotf[pl.ds(2 * cols * k + i, cols, stride=2), :] = sc[i, pl.ds(k + 2, cols, stride=8), :]
    score_ref[...] = cotf[pl.ds(0, 8 * cols), :].astype(BF)
    for k in range(4):
        here = pl.ds(k * cols, cols)
        lo, mid_lo, mid_hi, hi = (gs[i, pl.ds(k, cols, stride=4), :] for i in range(4))
        g_ref[here, pl.ds(0, 128)] = mid_lo
        g_ref[here, pl.ds(128, 128)] = mid_hi
        far_out[here, :] = jnp.where(first, lo, hi).astype(BF)
        near_out[here, :] = jnp.where(first, hi, lo).astype(BF)


def conv(cols, core, w_out, weights, own, up, dn, far, near, cot):
    vmem = pl.BlockSpec(memory_space=pltpu.VMEM)
    smem = pl.BlockSpec(memory_space=pltpu.SMEM)
    n = 4 * cols
    return pl.pallas_call(
        functools.partial(conv_kernel, cols),
        out_shape=(
            jax.ShapeDtypeStruct((8 * cols, 128), BF),
            jax.ShapeDtypeStruct((n, 256), F32),
            jax.ShapeDtypeStruct((n, 128), BF),
            jax.ShapeDtypeStruct((n, 128), BF),
        ),
        in_specs=[smem, smem] + [vmem] * 9,
        out_specs=(vmem,) * 4,
        scratch_shapes=[
            pltpu.VMEM((4, 8 * cols, 128), F32),
            pltpu.VMEM(((cols + 2) * TAPS * 8, 256), BF),
            pltpu.VMEM((12 * cols, 128), F32),
            pltpu.VMEM((2, 8 * cols, 128), F32),
            pltpu.VMEM(((cols + 2) * 64, 256), BF),
            pltpu.VMEM((2, 8 * cols, 128), F32),
            pltpu.VMEM((4, 4 * cols, 128), F32),
        ],
        compiler_params=pltpu.CompilerParams(vmem_limit_bytes=40 * 2**20),
        cost_estimate=pl.CostEstimate(flops=4 * 10**9, transcendentals=10**7, bytes_accessed=4 * 10**6),
    )(core, w_out, *weights, own, up, dn, far, near, cot)


def filters(w_src, b_src, w_tgt, b_tgt, first_row, total_rows):
    both = jnp.einsum(
        "opde,pab->odeab", w_tgt.astype(F32), w_src.astype(F32), precision=lax.Precision.HIGHEST
    )
    up = np.zeros((3, 8, 8), np.float32)
    for d in range(3):
        for m in range(1, 7):
            up[d, m, m + d - 1] = 1
    flat = jnp.pad(both.reshape(8, 3, 3, 9), ((0, 0), (0, 0), (0, 0), (0, TAPS - 9)))
    wf = (0.5 * jnp.einsum("odex,dmk->omexk", flat, up)).reshape(64, 3 * TAPS * 8).astype(BF)
    back = np.zeros((3, 4, 8), np.float32)
    side = np.zeros((3, 2, 4), np.float32)
    for d in range(3):
        for k in range(4):
            back[d, k, k + 3 - d] = 1
        for s in range(2):
            side[d, s, s + 2 - d] = 1
    spots = np.einsum("dkm,esl->desklm", back, side)
    wb = jnp.einsum("odeab,desklm->baskyom".replace("y", "l"), both, spots).reshape(72, 256).astype(BF)
    lift = jnp.einsum(
        "opde,p->ode", w_tgt.astype(F32), b_src, precision=lax.Precision.HIGHEST
    )
    row = first_row - 2 + jnp.arange(8)
    inside = ((row >= 0) & (row < total_rows)).astype(F32)
    edge = np.ones((3, 3), np.float32)
    edge[0, 0] = 0
    edge[2, 2] = 0
    along = jnp.einsum("ode,te->tod", lift, edge, precision=lax.Precision.HIGHEST)
    reach = jnp.einsum("dmk,k->md", up, inside, precision=lax.Precision.HIGHEST)
    bias = b_tgt[None, :, None] + jnp.einsum("tod,md->tom", along, reach, precision=lax.Precision.HIGHEST)
    bias = jnp.broadcast_to((0.5 * bias).reshape(192, 1), (192, 256))
    return wf, wb, bias


SRC = ("z", "core")
TGT = ("y", "x", "zh")
SIZES = {"z": 4, "core": 2, "y": 4, "x": 4, "zh": 2}


def moved(x, move):
    n_src, n_tgt = lax.axis_size(SRC), lax.axis_size(TGT)
    pairs = []
    for a in range(n_src):
        for b in range(n_tgt):
            c, d = move(a, b)
            if 0 <= c < n_src and 0 <= d < n_tgt:
                pairs.append((a * n_tgt + b, c * n_tgt + d))
    return lax.ppermute(x, SRC + TGT, pairs)


def far_row(a, b):
    return (a + 1 if a % 2 else a - 1, b)


def near_row(a, b):
    return (a ^ 1, b)


def body(src_feat, tgt_feat, w_src, b_src, w_tgt, b_tgt, w_out, cotangent):
    rows_k, cols, rows_i, cols_j = cotangent.shape
    chans = tgt_feat.shape[2]
    scale = chans ** (-0.5)
    n_src, n_tgt = lax.axis_size(SRC), lax.axis_size(TGT)
    t, z, core, zh = (lax.axis_index(a) for a in (TGT, "z", "core", "zh"))
    first = core == 0
    block = chans // n_tgt
    pixels = rows_i * cols_j

    weights = filters(w_src, b_src, w_tgt, b_tgt, t * rows_k, rows_k * n_tgt)
    tgt_flat = tgt_feat.reshape(rows_k * cols, chans)

    piece = src_feat.reshape(pixels, block).T
    src_t = lax.all_to_all(
        jnp.broadcast_to(piece[None], (n_tgt, block, pixels)), TGT, 0, 0, tiled=True
    ).reshape(chans, pixels)

    raw = jnp.dot(tgt_flat, src_t, preferred_element_type=F32)
    own = (raw * scale).astype(BF)
    cot = cotangent.reshape(rows_k * cols * rows_i, cols_j)

    def edge(k, cot_k):
        part = own[k * cols:(k + 2) * cols]
        line = cot[cot_k * cols * rows_i:(cot_k + 1) * cols * rows_i]
        return jnp.concatenate([part[:, :cols_j], part[:, cols_j:], line], 0)

    up = moved(edge(rows_k - 2, rows_k - 1), lambda a, b: (a, b + 1))
    dn = moved(edge(0, 0), lambda a, b: (a, b - 1))
    two = 2 * cols
    low = jnp.concatenate([up[:two], own[:, :cols_j], dn[:two]], 0)
    high = jnp.concatenate([up[two:2 * two], own[:, cols_j:], dn[two:2 * two]], 0)
    near = moved(jnp.where(first, high, low), near_row)
    far = moved(jnp.where(first, low, high), far_row)

    score, g_own, to_far, to_near = conv(
        cols, core.astype(jnp.int32)[None], w_out, weights, own, up, dn, far, near, cot
    )
    from_near = moved(to_near, near_row)
    from_far = moved(to_far, far_row)
    g = jnp.concatenate(
        [
            g_own[:, :cols_j] + jnp.where(first, from_far, from_near).astype(F32),
            g_own[:, cols_j:] + jnp.where(first, from_near, from_far).astype(F32),
        ],
        1,
    ).astype(BF)

    cut = src_t.reshape(n_src, chans // n_src, pixels)
    hops = n_src // 2

    def blocks(side):
        return jnp.concatenate(
            [lax.dynamic_index_in_dim(cut, (z ^ m) * 2 + side, 0, False) for m in range(hops)], 0
        )

    over = (((1,), (1,)), ((), ()))
    other = lax.dot_general(g, blocks(1 - core), over, preferred_element_type=F32) * scale
    got = moved(other.astype(BF), near_row)
    mine = lax.dot_general(g, blocks(core), over, preferred_element_type=F32) * scale
    both = mine + got.astype(F32)
    width = chans // n_src
    total = both[:, :width]
    for m in range(1, hops):
        total = total + moved(
            both[:, m * width:(m + 1) * width].astype(BF), lambda a, b, m=m: (a ^ (2 * m), b)
        ).astype(F32)
    grad_tgt = total.reshape(rows_k, cols, width)

    part = lax.dot_general(tgt_flat, g, (((0,), (0,)), ((), ())), preferred_element_type=F32) * scale
    plane = n_tgt // 2
    parts = lax.all_to_all(
        part.astype(BF).reshape(plane, 2 * block, pixels), ("y", "x"), 0, 0, tiled=True
    )
    halves = jnp.sum(parts.astype(F32), 0).reshape(2, block, pixels)
    keep = lax.dynamic_index_in_dim(halves, zh, 0, False)
    send = lax.dynamic_index_in_dim(halves, 1 - zh, 0, False)
    grad_src = keep + moved(send.astype(BF), lambda a, b: (a, b ^ 1)).astype(F32)
    return (score.reshape(cotangent.shape), grad_src.reshape(block, rows_i, cols_j), grad_tgt)


def solution(mesh):
    fine = jax.sharding.Mesh(mesh.devices.reshape(tuple(SIZES.values())), tuple(SIZES))
    placed = (
        P(SRC, None, TGT),
        P(TGT, None, None),
        P(),
        P(),
        P(),
        P(),
        P(),
        P(TGT, None, SRC, None),
    )
    return jax.shard_map(
        body,
        mesh=fine,
        in_specs=placed,
        out_specs=(P(TGT, None, SRC, None), P(TGT, SRC, None), P(TGT, None, SRC)),
        check_vma=False,
    )
```

```python
import functools

import jax
import jax.numpy as jnp
import numpy as np
from jax import lax
from jax.experimental import pallas as pl
from jax.experimental.pallas import tpu as pltpu
from jax.sharding import PartitionSpec as P

BF = jnp.bfloat16
F32 = jnp.float32
TAPS = 10


def shift_lanes(v, by):
    n = v.shape[1]
    lane = lax.broadcasted_iota(jnp.int32, v.shape, 1)
    edge = 0 if by == 1 else n - 1
    return jnp.where(lane == edge, 0.0, pltpu.roll(v, by % n, 1))


def conv_kernel(
    cols,
    scale, spot_ref, wf_ref, wb_ref, bias_ref, tgt_ref, src_ref, far_ref, near_ref, up_ref, dn_ref, cot_ref,
    *more,
):
    n_more = len(more) - 11
    halo_refs = more[:n_more]
    score_ref, g_ref, far_out, near_out, cs, rows, cotf, cots, gp, sc, gs = more[n_more:]
    hop, core = spot_ref[0], spot_ref[1]
    first = core == 0

    def put(part, at, ks):
        part = (part * scale).astype(BF).astype(F32)
        for n, k in enumerate(ks):
            cs[at, pl.ds(k, cols, stride=8), :] = part[n * cols:(n + 1) * cols]

    def fill(product, ks):
        far, near = product(far_ref), product(near_ref)
        put(jnp.where(first, far, near), 0, ks)
        put(jnp.where(first, near, far), 3, ks)
        mid = product(src_ref)
        put(mid[:, :128], 1, ks)
        put(mid[:, 128:], 2, ks)

    def over_all(ref):
        return jnp.dot(tgt_ref[...], ref[...], preferred_element_type=F32)

    def over_pieces(ref):
        total = None
        for n, piece in enumerate(halo_refs):
            block = (hop ^ (n // 2)) * 2 + (core ^ (n % 2))
            part = jnp.dot(
                piece[...], ref[pl.ds(pl.multiple_of(block * 128, 128), 128), :], preferred_element_type=F32
            )
            total = part if total is None else total + part
        return total

    fill(over_all, (2, 3, 4, 5))
    fill(over_pieces, (0, 1, 6, 7))
    zeros = jnp.zeros((cols, 128), F32)
    cotf[pl.ds(0, 2 * cols), :] = up_ref[pl.ds(2 * cols, 2 * cols), :].astype(F32)
    cotf[pl.ds(2 * cols, 8 * cols), :] = cot_ref[...].astype(F32)
    cotf[pl.ds(10 * cols, 2 * cols), :] = dn_ref[pl.ds(2 * cols, 2 * cols), :].astype(F32)
    for i in range(2):
        cots[i, pl.ds(0, cols, stride=8), :] = zeros
        cots[i, pl.ds(7, cols, stride=8), :] = zeros
        for k in range(6):
            cots[i, pl.ds(k + 1, cols, stride=8), :] = cotf[pl.ds(2 * cols * k + i, cols, stride=2), :]

    group = TAPS * 8
    for end in (0, cols + 1):
        rows[pl.ds(end * group, group), :] = jnp.zeros((group, 256), BF)
        gp[pl.ds(end * 64, 64), :] = jnp.zeros((64, 256), BF)

    def spread(l, _):
        at = pl.multiple_of(l * 8, 8)
        taps = []
        for i in range(4):
            v = cs[i, pl.ds(at, 8), :]
            taps.append((shift_lanes(v, 1), v, shift_lanes(v, -1)))
        for i in range(2):
            block = [taps[i + a][b] for a in range(3) for b in range(3)]
            block.append(jnp.zeros((8, 128), F32))
            rows[pl.ds(pl.multiple_of((l + 1) * group, 16), group), pl.ds(i * 128, 128)] = jnp.concatenate(block, 0).astype(BF)
        return 0

    lax.fori_loop(0, cols, spread, 0, unroll=48)

    wf = wf_ref[...]
    wb = wb_ref[...]

    def forward(l, _):
        kind = jnp.where(l == 0, 0, jnp.where(l == cols - 1, 2, 1))
        window = rows[pl.ds(pl.multiple_of(l * group, 16), 3 * group), :]
        u = jnp.dot(wf, window, preferred_element_type=F32)
        u = u + bias_ref[pl.ds(pl.multiple_of(kind * 64, 64), 64), :]
        th = jnp.tanh(u)
        q = u * th
        g = (1.0 + u) + th * (1.0 - q)
        s = u + q
        at = pl.multiple_of(l * 8, 8)
        cot = jnp.concatenate([cots[0, pl.ds(at, 8), :], cots[1, pl.ds(at, 8), :]], 1)
        total = jnp.zeros((8, 256), F32)
        out = []
        for o in range(8):
            w = bias_ref[pl.ds(192 + o * 8, 8), :]
            total = total + w * s[o * 8:o * 8 + 8]
            out.append(g[o * 8:o * 8 + 8] * (cot * (0.5 * w)))
        gp[pl.ds(pl.multiple_of((l + 1) * 64, 64), 64), :] = jnp.concatenate(out, 0).astype(BF)
        sc[0, pl.ds(at, 8), :] = total[:, :128]
        sc[1, pl.ds(at, 8), :] = total[:, 128:]
        return 0

    lax.fori_loop(0, cols, forward, 0, unroll=96)

    def backward(m, _):
        window = gp[pl.ds(pl.multiple_of(m * 128, 128), 256), :]
        t = jnp.dot(wb, window, preferred_element_type=F32)
        at = pl.multiple_of(m * 8, 8)
        for io in range(4):
            part = []
            for b in range(3):
                pieces = []
                for a in range(3):
                    i = io - a
                    if 0 <= i < 2:
                        pieces.append(t[(b * 3 + a) * 8:(b * 3 + a) * 8 + 8, i * 128:(i + 1) * 128])
                part.append(functools.reduce(jnp.add, pieces))
            gs[io, pl.ds(at, 8), :] = shift_lanes(part[0], -1) + part[1] + shift_lanes(part[2], 1)
        return 0

    lax.fori_loop(0, cols // 2, backward, 0, unroll=48)

    for k in range(4):
        for i in range(2):
            cotf[pl.ds(2 * cols * k + i, cols, stride=2), :] = sc[i, pl.ds(k + 2, cols, stride=8), :]
    score_ref[...] = cotf[pl.ds(0, 8 * cols), :].astype(BF)
    for k in range(4):
        here = pl.ds(k * cols, cols)
        lo, mid_lo, mid_hi, hi = (gs[i, pl.ds(k, cols, stride=4), :] for i in range(4))
        g_ref[here, pl.ds(0, 128)] = mid_lo
        g_ref[here, pl.ds(128, 128)] = mid_hi
        far_out[here, :] = jnp.where(first, lo, hi).astype(BF)
        near_out[here, :] = jnp.where(first, hi, lo).astype(BF)


def conv(cols, scale, spot, weights, tgt, src, far, near, up, dn, cot, halos):
    vmem = pl.BlockSpec(memory_space=pltpu.VMEM)
    smem = pl.BlockSpec(memory_space=pltpu.SMEM)
    n = 4 * cols
    return pl.pallas_call(
        functools.partial(conv_kernel, cols, scale),
        out_shape=(
            jax.ShapeDtypeStruct((8 * cols, 128), BF),
            jax.ShapeDtypeStruct((n, 256), F32),
            jax.ShapeDtypeStruct((n, 128), BF),
            jax.ShapeDtypeStruct((n, 128), BF),
        ),
        in_specs=[smem] + [vmem] * (10 + len(halos)),
        out_specs=(vmem,) * 4,
        scratch_shapes=[
            pltpu.VMEM((4, 8 * cols, 128), F32),
            pltpu.VMEM(((cols + 2) * TAPS * 8, 256), BF),
            pltpu.VMEM((12 * cols, 128), F32),
            pltpu.VMEM((2, 8 * cols, 128), F32),
            pltpu.VMEM(((cols + 2) * 64, 256), BF),
            pltpu.VMEM((2, 8 * cols, 128), F32),
            pltpu.VMEM((4, 4 * cols, 128), F32),
        ],
        compiler_params=pltpu.CompilerParams(vmem_limit_bytes=40 * 2**20),
        cost_estimate=pl.CostEstimate(flops=4 * 10**9, transcendentals=10**7, bytes_accessed=4 * 10**6),
    )(spot, *weights, tgt, src, far, near, up, dn, cot, *halos)


def filters(w_src, b_src, w_tgt, b_tgt, w_out, first_row, total_rows):
    both = jnp.einsum(
        "opde,pab->odeab", w_tgt.astype(F32), w_src.astype(F32), precision=lax.Precision.HIGHEST
    )
    up = np.zeros((3, 8, 8), np.float32)
    for d in range(3):
        for m in range(1, 7):
            up[d, m, m + d - 1] = 1
    flat = jnp.pad(both.reshape(8, 3, 3, 9), ((0, 0), (0, 0), (0, 0), (0, TAPS - 9)))
    wf = (0.5 * jnp.einsum("odex,dmk->omexk", flat, up)).reshape(64, 3 * TAPS * 8).astype(BF)
    back = np.zeros((3, 4, 8), np.float32)
    side = np.zeros((3, 2, 4), np.float32)
    for d in range(3):
        for k in range(4):
            back[d, k, k + 3 - d] = 1
        for s in range(2):
            side[d, s, s + 2 - d] = 1
    spots = np.einsum("dkm,esl->desklm", back, side)
    wb = jnp.einsum("odeab,desklm->baskyom".replace("y", "l"), both, spots).reshape(72, 256).astype(BF)
    lift = jnp.einsum(
        "opde,p->ode", w_tgt.astype(F32), b_src, precision=lax.Precision.HIGHEST
    )
    row = first_row - 2 + jnp.arange(8)
    inside = ((row >= 0) & (row < total_rows)).astype(F32)
    edge = np.ones((3, 3), np.float32)
    edge[0, 0] = 0
    edge[2, 2] = 0
    along = jnp.einsum("ode,te->tod", lift, edge, precision=lax.Precision.HIGHEST)
    reach = jnp.einsum("dmk,k->md", up, inside, precision=lax.Precision.HIGHEST)
    bias = b_tgt[None, :, None] + jnp.einsum("tod,md->tom", along, reach, precision=lax.Precision.HIGHEST)
    bias = jnp.concatenate([(0.5 * bias).reshape(192), jnp.repeat(w_out, 8)])
    bias = jnp.broadcast_to(bias[:, None], (256, 256))
    return wf, wb, bias


SRC = ("z", "core")
TGT = ("y", "x", "zh")
SIZES = {"z": 4, "core": 2, "y": 4, "x": 4, "zh": 2}


def moved(x, move):
    n_src, n_tgt = lax.axis_size(SRC), lax.axis_size(TGT)
    pairs = []
    for a in range(n_src):
        for b in range(n_tgt):
            c, d = move(a, b)
            if 0 <= c < n_src and 0 <= d < n_tgt:
                pairs.append((a * n_tgt + b, c * n_tgt + d))
    return lax.ppermute(x, SRC + TGT, pairs)


def far_row(a, b):
    return (a + 1 if a % 2 else a - 1, b)


def near_row(a, b):
    return (a ^ 1, b)


def body(src_feat, tgt_feat, w_src, b_src, w_tgt, b_tgt, w_out, cotangent):
    rows_k, cols, rows_i, cols_j = cotangent.shape
    chans = tgt_feat.shape[2]
    scale = chans ** (-0.5)
    n_src, n_tgt = lax.axis_size(SRC), lax.axis_size(TGT)
    s, t, z, core, zh = (lax.axis_index(a) for a in (SRC, TGT, "z", "core", "zh"))
    first = core == 0
    block = chans // n_tgt
    pixels = rows_i * cols_j

    weights = filters(w_src, b_src, w_tgt, b_tgt, w_out, t * rows_k, rows_k * n_tgt)
    tgt_flat = tgt_feat.reshape(rows_k * cols, chans)
    cot = cotangent.reshape(rows_k * cols * rows_i, cols_j)
    width = chans // n_src
    hops = n_src // 2

    def edge(k, cot_k):
        part = lax.dynamic_slice_in_dim(tgt_flat[k * cols:(k + 2) * cols], s * width, width, 1)
        return jnp.concatenate([part, cot[cot_k * cols * rows_i:(cot_k + 1) * cols * rows_i]], 0)

    up = moved(edge(rows_k - 2, rows_k - 1), lambda a, b: (a, b + 1))
    dn = moved(edge(0, 0), lambda a, b: (a, b - 1))
    two = 2 * cols
    share = jnp.concatenate([up[:two], dn[:two]], 0)
    halos = []
    for m in range(hops):
        mine = share if m == 0 else moved(share, lambda a, b, m=m: (a ^ (2 * m), b))
        halos += [mine, moved(mine, near_row)]

    piece = src_feat.reshape(pixels, block).T
    other = moved(piece, lambda a, b: (a, b ^ 1))
    pair = jnp.where(zh == 0, jnp.concatenate([piece, other], 0), jnp.concatenate([other, piece], 0))
    plane = n_tgt // 2
    src_t = lax.all_to_all(
        jnp.broadcast_to(pair[None], (plane, 2 * block, pixels)), ("y", "x"), 0, 0, tiled=True
    ).reshape(chans, pixels)
    low, high = src_t[:, :cols_j], src_t[:, cols_j:]
    near = moved(jnp.where(first, high, low), near_row)
    far = moved(jnp.where(first, low, high), far_row)

    spot = jnp.stack([z, core]).astype(jnp.int32)
    score, g_own, to_far, to_near = conv(
        cols, scale, spot, weights, tgt_flat, src_t, far, near, up, dn, cot, halos
    )
    from_near = moved(to_near, near_row)
    from_far = moved(to_far, far_row)
    g = jnp.concatenate(
        [
            g_own[:, :cols_j] + jnp.where(first, from_far, from_near).astype(F32),
            g_own[:, cols_j:] + jnp.where(first, from_near, from_far).astype(F32),
        ],
        1,
    ).astype(BF)

    cut = src_t.reshape(n_src, width, pixels)

    def blocks(side):
        return jnp.concatenate(
            [lax.dynamic_index_in_dim(cut, (z ^ m) * 2 + side, 0, False) for m in range(hops)], 0
        )

    over = (((1,), (1,)), ((), ()))
    other = lax.dot_general(g, blocks(1 - core), over, preferred_element_type=F32) * scale
    got = moved(other.astype(BF), near_row)
    mine = lax.dot_general(g, blocks(core), over, preferred_element_type=F32) * scale
    both = mine + got.astype(F32)
    total = both[:, :width]
    for m in range(1, hops):
        total = total + moved(
            both[:, m * width:(m + 1) * width].astype(BF), lambda a, b, m=m: (a ^ (2 * m), b)
        ).astype(F32)
    grad_tgt = total.reshape(rows_k, cols, width)

    part = lax.dot_general(tgt_flat, g, (((0,), (0,)), ((), ())), preferred_element_type=F32) * scale
    parts = lax.all_to_all(
        part.astype(BF).reshape(plane, 2 * block, pixels), ("y", "x"), 0, 0, tiled=True
    )
    halves = jnp.sum(parts.astype(F32), 0).reshape(2, block, pixels)
    keep = lax.dynamic_index_in_dim(halves, zh, 0, False)
    send = lax.dynamic_index_in_dim(halves, 1 - zh, 0, False)
    grad_src = keep + moved(send.astype(BF), lambda a, b: (a, b ^ 1)).astype(F32)
    return (score.reshape(cotangent.shape), grad_src.reshape(block, rows_i, cols_j), grad_tgt)


def solution(mesh):
    fine = jax.sharding.Mesh(mesh.devices.reshape(tuple(SIZES.values())), tuple(SIZES))
    placed = (
        P(SRC, None, TGT),
        P(TGT, None, None),
        P(),
        P(),
        P(),
        P(),
        P(),
        P(TGT, None, SRC, None),
    )
    return jax.shard_map(
        body,
        mesh=fine,
        in_specs=placed,
        out_specs=(P(TGT, None, SRC, None), P(TGT, SRC, None), P(TGT, None, SRC)),
        check_vma=False,
    )
```

```python
import functools

import jax
import jax.numpy as jnp
import numpy as np
from jax import lax
from jax.experimental import pallas as pl
from jax.experimental.pallas import tpu as pltpu
from jax.sharding import PartitionSpec as P

BF = jnp.bfloat16
F32 = jnp.float32
TAPS = 10


def shift_lanes(v, by):
    n = v.shape[1]
    lane = lax.broadcasted_iota(jnp.int32, v.shape, 1)
    edge = 0 if by == 1 else n - 1
    return jnp.where(lane == edge, 0.0, pltpu.roll(v, by % n, 1))


def conv_kernel(
    cols,
    scale, spot_ref, wf_ref, wb_ref, bias_ref, tgt_ref, src_ref, far_ref, near_ref, pair_ref, next_ref, cot_ref,
    *more,
):
    n_more = len(more) - 11
    halo_refs = more[:n_more]
    score_ref, g_ref, far_out, near_out, cs, rows, cotf, cots, gp, sc, gs = more[n_more:]
    hop, core = spot_ref[0], spot_ref[1]
    first = core == 0
    even = spot_ref[2] == 0

    def put(part, at, ks):
        part = (part * scale).astype(BF).astype(F32)
        for n, k in enumerate(ks):
            cs[at, pl.ds(k, cols, stride=8), :] = part[n * cols:(n + 1) * cols]

    def fill(product, ks):
        far, near = product(far_ref), product(near_ref)
        put(jnp.where(first, far, near), 0, ks)
        put(jnp.where(first, near, far), 3, ks)
        mid = product(src_ref)
        put(mid[:, :128], 1, ks)
        put(mid[:, 128:], 2, ks)

    def over_all(ref):
        return jnp.dot(tgt_ref[...], ref[...], preferred_element_type=F32)

    def over_pieces(ref):
        total = None
        for n, piece in enumerate(halo_refs):
            block = (hop ^ (n // 2)) * 2 + (core ^ (n % 2))
            part = jnp.dot(
                piece[...], ref[pl.ds(pl.multiple_of(block * 128, 128), 128), :], preferred_element_type=F32
            )
            total = part if total is None else total + part
        pair, next_ = total[:2 * cols], total[2 * cols:]
        return jnp.concatenate([jnp.where(even, next_, pair), jnp.where(even, pair, next_)], 0)

    fill(over_all, (2, 3, 4, 5))
    fill(over_pieces, (0, 1, 6, 7))
    zeros = jnp.zeros((cols, 128), F32)
    line = pl.ds(2 * cols, 2 * cols)
    pair, next_ = pair_ref[line, :].astype(F32), next_ref[line, :].astype(F32)
    cotf[pl.ds(0, 2 * cols), :] = jnp.where(even, next_, pair)
    cotf[pl.ds(2 * cols, 8 * cols), :] = cot_ref[...].astype(F32)
    cotf[pl.ds(10 * cols, 2 * cols), :] = jnp.where(even, pair, next_)
    for i in range(2):
        cots[i, pl.ds(0, cols, stride=8), :] = zeros
        cots[i, pl.ds(7, cols, stride=8), :] = zeros
        for k in range(6):
            cots[i, pl.ds(k + 1, cols, stride=8), :] = cotf[pl.ds(2 * cols * k + i, cols, stride=2), :]

    group = TAPS * 8
    for end in (0, cols + 1):
        rows[pl.ds(end * group, group), :] = jnp.zeros((group, 256), BF)
        gp[pl.ds(end * 64, 64), :] = jnp.zeros((64, 256), BF)

    def spread(l, _):
        at = pl.multiple_of(l * 8, 8)
        taps = []
        for i in range(4):
            v = cs[i, pl.ds(at, 8), :]
            taps.append((shift_lanes(v, 1), v, shift_lanes(v, -1)))
        for i in range(2):
            block = [taps[i + a][b] for a in range(3) for b in range(3)]
            block.append(jnp.zeros((8, 128), F32))
            rows[pl.ds(pl.multiple_of((l + 1) * group, 16), group), pl.ds(i * 128, 128)] = jnp.concatenate(block, 0).astype(BF)
        return 0

    lax.fori_loop(0, cols, spread, 0, unroll=48)

    wf = wf_ref[...]
    wb = wb_ref[...]

    def forward(l, _):
        kind = jnp.where(l == 0, 0, jnp.where(l == cols - 1, 2, 1))
        window = rows[pl.ds(pl.multiple_of(l * group, 16), 3 * group), :]
        u = jnp.dot(wf, window, preferred_element_type=F32)
        u = u + bias_ref[pl.ds(pl.multiple_of(kind * 64, 64), 64), :]
        th = jnp.tanh(u)
        q = u * th
        g = (1.0 + u) + th * (1.0 - q)
        s = u + q
        at = pl.multiple_of(l * 8, 8)
        cot = jnp.concatenate([cots[0, pl.ds(at, 8), :], cots[1, pl.ds(at, 8), :]], 1)
        total = jnp.zeros((8, 256), F32)
        out = []
        for o in range(8):
            w = bias_ref[pl.ds(192 + o * 8, 8), :]
            total = total + w * s[o * 8:o * 8 + 8]
            out.append(g[o * 8:o * 8 + 8] * (cot * (0.5 * w)))
        gp[pl.ds(pl.multiple_of((l + 1) * 64, 64), 64), :] = jnp.concatenate(out, 0).astype(BF)
        sc[0, pl.ds(at, 8), :] = total[:, :128]
        sc[1, pl.ds(at, 8), :] = total[:, 128:]
        return 0

    lax.fori_loop(0, cols, forward, 0, unroll=96)

    def backward(m, _):
        window = gp[pl.ds(pl.multiple_of(m * 128, 128), 256), :]
        t = jnp.dot(wb, window, preferred_element_type=F32)
        at = pl.multiple_of(m * 8, 8)
        for io in range(4):
            part = []
            for b in range(3):
                pieces = []
                for a in range(3):
                    i = io - a
                    if 0 <= i < 2:
                        pieces.append(t[(b * 3 + a) * 8:(b * 3 + a) * 8 + 8, i * 128:(i + 1) * 128])
                part.append(functools.reduce(jnp.add, pieces))
            gs[io, pl.ds(at, 8), :] = shift_lanes(part[0], -1) + part[1] + shift_lanes(part[2], 1)
        return 0

    lax.fori_loop(0, cols // 2, backward, 0, unroll=48)

    for k in range(4):
        for i in range(2):
            cotf[pl.ds(2 * cols * k + i, cols, stride=2), :] = sc[i, pl.ds(k + 2, cols, stride=8), :]
    score_ref[...] = cotf[pl.ds(0, 8 * cols), :].astype(BF)
    for k in range(4):
        here = pl.ds(k * cols, cols)
        lo, mid_lo, mid_hi, hi = (gs[i, pl.ds(k, cols, stride=4), :] for i in range(4))
        g_ref[here, pl.ds(0, 128)] = mid_lo
        g_ref[here, pl.ds(128, 128)] = mid_hi
        far_out[here, :] = jnp.where(first, lo, hi).astype(BF)
        near_out[here, :] = jnp.where(first, hi, lo).astype(BF)


def conv(cols, scale, spot, weights, tgt, src, far, near, pair, next_, cot, halos):
    vmem = pl.BlockSpec(memory_space=pltpu.VMEM)
    smem = pl.BlockSpec(memory_space=pltpu.SMEM)
    n = 4 * cols
    return pl.pallas_call(
        functools.partial(conv_kernel, cols, scale),
        out_shape=(
            jax.ShapeDtypeStruct((8 * cols, 128), BF),
            jax.ShapeDtypeStruct((n, 256), F32),
            jax.ShapeDtypeStruct((n, 128), BF),
            jax.ShapeDtypeStruct((n, 128), BF),
        ),
        in_specs=[smem] + [vmem] * (10 + len(halos)),
        out_specs=(vmem,) * 4,
        scratch_shapes=[
            pltpu.VMEM((4, 8 * cols, 128), F32),
            pltpu.VMEM(((cols + 2) * TAPS * 8, 256), BF),
            pltpu.VMEM((12 * cols, 128), F32),
            pltpu.VMEM((2, 8 * cols, 128), F32),
            pltpu.VMEM(((cols + 2) * 64, 256), BF),
            pltpu.VMEM((2, 8 * cols, 128), F32),
            pltpu.VMEM((4, 4 * cols, 128), F32),
        ],
        compiler_params=pltpu.CompilerParams(vmem_limit_bytes=40 * 2**20),
        cost_estimate=pl.CostEstimate(flops=4 * 10**9, transcendentals=10**7, bytes_accessed=4 * 10**6),
    )(spot, *weights, tgt, src, far, near, pair, next_, cot, *halos)


def filters(w_src, b_src, w_tgt, b_tgt, w_out, first_row, total_rows):
    both = jnp.einsum(
        "opde,pab->odeab", w_tgt.astype(F32), w_src.astype(F32), precision=lax.Precision.HIGHEST
    )
    up = np.zeros((3, 8, 8), np.float32)
    for d in range(3):
        for m in range(1, 7):
            up[d, m, m + d - 1] = 1
    flat = jnp.pad(both.reshape(8, 3, 3, 9), ((0, 0), (0, 0), (0, 0), (0, TAPS - 9)))
    wf = (0.5 * jnp.einsum("odex,dmk->omexk", flat, up)).reshape(64, 3 * TAPS * 8).astype(BF)
    back = np.zeros((3, 4, 8), np.float32)
    side = np.zeros((3, 2, 4), np.float32)
    for d in range(3):
        for k in range(4):
            back[d, k, k + 3 - d] = 1
        for s in range(2):
            side[d, s, s + 2 - d] = 1
    spots = np.einsum("dkm,esl->desklm", back, side)
    wb = jnp.einsum("odeab,desklm->baskyom".replace("y", "l"), both, spots).reshape(72, 256).astype(BF)
    lift = jnp.einsum(
        "opde,p->ode", w_tgt.astype(F32), b_src, precision=lax.Precision.HIGHEST
    )
    row = first_row - 2 + jnp.arange(8)
    inside = ((row >= 0) & (row < total_rows)).astype(F32)
    edge = np.ones((3, 3), np.float32)
    edge[0, 0] = 0
    edge[2, 2] = 0
    along = jnp.einsum("ode,te->tod", lift, edge, precision=lax.Precision.HIGHEST)
    reach = jnp.einsum("dmk,k->md", up, inside, precision=lax.Precision.HIGHEST)
    bias = b_tgt[None, :, None] + jnp.einsum("tod,md->tom", along, reach, precision=lax.Precision.HIGHEST)
    bias = jnp.concatenate([(0.5 * bias).reshape(192), jnp.repeat(w_out, 8)])
    bias = jnp.broadcast_to(bias[:, None], (256, 256))
    return wf, wb, bias


SRC = ("z", "core")
TGT = ("y", "x", "zh")
SIZES = {"z": 4, "core": 2, "y": 4, "x": 4, "zh": 2}


def moved(x, move):
    n_src, n_tgt = lax.axis_size(SRC), lax.axis_size(TGT)
    pairs = []
    for a in range(n_src):
        for b in range(n_tgt):
            c, d = move(a, b)
            if 0 <= c < n_src and 0 <= d < n_tgt:
                pairs.append((a * n_tgt + b, c * n_tgt + d))
    return lax.ppermute(x, SRC + TGT, pairs)


def far_row(a, b):
    return (a + 1 if a % 2 else a - 1, b)


def near_row(a, b):
    return (a ^ 1, b)


def body(src_feat, tgt_feat, w_src, b_src, w_tgt, b_tgt, w_out, cotangent):
    rows_k, cols, rows_i, cols_j = cotangent.shape
    chans = tgt_feat.shape[2]
    scale = chans ** (-0.5)
    n_src, n_tgt = lax.axis_size(SRC), lax.axis_size(TGT)
    s, t, z, core, zh = (lax.axis_index(a) for a in (SRC, TGT, "z", "core", "zh"))
    first = core == 0
    block = chans // n_tgt
    pixels = rows_i * cols_j

    tgt_flat = tgt_feat.reshape(rows_k * cols, chans)
    cot = cotangent.reshape(rows_k * cols * rows_i, cols_j)
    width = chans // n_src
    hops = n_src // 2

    piece = src_feat.reshape(pixels, block).T
    line = cols * rows_i

    def edge(last, *extra):
        k = jnp.where(last, rows_k - 2, 0)
        part = lax.dynamic_slice(tgt_feat, (k, 0, s * width), (2, cols, width)).reshape(2 * cols, width)
        k = jnp.where(last, rows_k - 1, 0)
        return jnp.concatenate([part, lax.dynamic_slice(cot, (k * line, 0), (line, cols_j)), *extra], 0)

    even = zh == 0
    pair = moved(edge(even, piece[:, :cols_j], piece[:, cols_j:]), lambda a, b: (a, b ^ 1))
    next_ = moved(edge(~even), lambda a, b: (a, b + 1 if b % 2 else b - 1))
    two = 2 * cols
    share = jnp.concatenate([pair[:two], next_[:two]], 0)
    shares = [share]
    for m in range(1, hops):
        shares.append(moved(share, lambda a, b, m=m: (a ^ (2 * m), b)))
    w_src, b_src, w_tgt, b_tgt, share = lax.optimization_barrier((w_src, b_src, w_tgt, b_tgt, share))
    weights = filters(w_src, b_src, w_tgt, b_tgt, w_out, t * rows_k, rows_k * n_tgt)

    start = two + line
    other = jnp.concatenate([pair[start:start + block], pair[start + block:]], 1)
    both = jnp.where(even, jnp.concatenate([piece, other], 0), jnp.concatenate([other, piece], 0))
    plane = n_tgt // 2
    src_t = lax.all_to_all(
        jnp.broadcast_to(both[None], (plane, 2 * block, pixels)), ("y", "x"), 0, 0, tiled=True
    ).reshape(chans, pixels)
    src_t, *shares = lax.optimization_barrier((src_t, *shares))
    halos = []
    for mine in shares:
        halos += [mine, moved(mine, near_row)]
    low, high = src_t[:, :cols_j], src_t[:, cols_j:]
    near = moved(jnp.where(first, high, low), near_row)
    far = moved(jnp.where(first, low, high), far_row)

    spot = jnp.stack([z, core, zh]).astype(jnp.int32)
    score, g_own, to_far, to_near = conv(
        cols, scale, spot, weights, tgt_flat, src_t, far, near, pair, next_, cot, halos
    )
    from_near = moved(to_near, near_row)
    from_far = moved(to_far, far_row)
    g = jnp.concatenate(
        [
            g_own[:, :cols_j] + jnp.where(first, from_far, from_near).astype(F32),
            g_own[:, cols_j:] + jnp.where(first, from_near, from_far).astype(F32),
        ],
        1,
    ).astype(BF)

    cut = src_t.reshape(n_src, width, pixels)

    def blocks(side):
        return jnp.concatenate(
            [lax.dynamic_index_in_dim(cut, (z ^ m) * 2 + side, 0, False) for m in range(hops)], 0
        )

    over = (((1,), (1,)), ((), ()))
    other = lax.dot_general(g, blocks(1 - core), over, preferred_element_type=F32) * scale
    got = moved(other.astype(BF), near_row)
    mine = lax.dot_general(g, blocks(core), over, preferred_element_type=F32) * scale
    both = mine + got.astype(F32)
    total = both[:, :width]
    for m in range(1, hops):
        total = total + moved(
            both[:, m * width:(m + 1) * width].astype(BF), lambda a, b, m=m: (a ^ (2 * m), b)
        ).astype(F32)
    grad_tgt = total.reshape(rows_k, cols, width)

    part = lax.dot_general(tgt_flat, g, (((0,), (0,)), ((), ())), preferred_element_type=F32) * scale
    parts = lax.all_to_all(
        part.astype(BF).reshape(plane, 2 * block, pixels), ("y", "x"), 0, 0, tiled=True
    )
    halves = jnp.sum(parts.astype(F32), 0).reshape(2, block, pixels)
    keep = lax.dynamic_index_in_dim(halves, zh, 0, False)
    send = lax.dynamic_index_in_dim(halves, 1 - zh, 0, False)
    grad_src = keep + moved(send.astype(BF), lambda a, b: (a, b ^ 1)).astype(F32)
    return (score.reshape(cotangent.shape), grad_src.reshape(block, rows_i, cols_j), grad_tgt)


def solution(mesh):
    fine = jax.sharding.Mesh(mesh.devices.reshape(tuple(SIZES.values())), tuple(SIZES))
    placed = (
        P(SRC, None, TGT),
        P(TGT, None, None),
        P(),
        P(),
        P(),
        P(),
        P(),
        P(TGT, None, SRC, None),
    )
    return jax.shard_map(
        body,
        mesh=fine,
        in_specs=placed,
        out_specs=(P(TGT, None, SRC, None), P(TGT, SRC, None), P(TGT, None, SRC)),
        check_vma=False,
    )
```

```python
import functools

import jax
import jax.numpy as jnp
import numpy as np
from jax import lax
from jax.experimental import pallas as pl
from jax.experimental.pallas import tpu as pltpu
from jax.sharding import PartitionSpec as P

BF = jnp.bfloat16
F32 = jnp.float32
TAPS = 10


def shift_lanes(v, by):
    n = v.shape[1]
    lane = lax.broadcasted_iota(jnp.int32, v.shape, 1)
    edge = 0 if by == 1 else n - 1
    return jnp.where(lane == edge, 0.0, pltpu.roll(v, by % n, 1))


def conv_kernel(
    cols,
    scale, spot_ref, wf_ref, wb_ref, bias_ref, tgt_ref, src_ref, far_ref, near_ref, pair_ref, next_ref, cot_ref,
    *more,
):
    n_more = len(more) - 11
    halo_refs = more[:n_more]
    score_ref, g_ref, far_out, near_out, cs, rows, cotf, cots, gp, sc, gs = more[n_more:]
    hop, core = spot_ref[0], spot_ref[1]
    first = core == 0
    even = spot_ref[2] == 0

    def put(part, at, ks):
        part = (part * scale).astype(BF).astype(F32)
        for n, k in enumerate(ks):
            cs[at, pl.ds(k, cols, stride=8), :] = part[n * cols:(n + 1) * cols]

    def fill(product, ks):
        far, near = product(far_ref), product(near_ref)
        put(jnp.where(first, far, near), 0, ks)
        put(jnp.where(first, near, far), 3, ks)
        mid = product(src_ref)
        put(mid[:, :128], 1, ks)
        put(mid[:, 128:], 2, ks)

    def over_all(ref):
        return jnp.dot(tgt_ref[...], ref[...], preferred_element_type=F32)

    def over_pieces(ref):
        total = None
        for n, piece in enumerate(halo_refs):
            block = (hop ^ (n // 2)) * 2 + (core ^ (n % 2))
            part = jnp.dot(
                piece[...], ref[pl.ds(pl.multiple_of(block * 128, 128), 128), :], preferred_element_type=F32
            )
            total = part if total is None else total + part
        pair, next_ = total[:2 * cols], total[2 * cols:]
        return jnp.concatenate([jnp.where(even, next_, pair), jnp.where(even, pair, next_)], 0)

    fill(over_all, (2, 3, 4, 5))
    fill(over_pieces, (0, 1, 6, 7))
    zeros = jnp.zeros((cols, 128), F32)
    line = pl.ds(2 * cols, 2 * cols)
    pair, next_ = pair_ref[line, :].astype(F32), next_ref[line, :].astype(F32)
    cotf[pl.ds(0, 2 * cols), :] = jnp.where(even, next_, pair)
    cotf[pl.ds(2 * cols, 8 * cols), :] = cot_ref[...].astype(F32)
    cotf[pl.ds(10 * cols, 2 * cols), :] = jnp.where(even, pair, next_)
    for i in range(2):
        cots[i, pl.ds(0, cols, stride=8), :] = zeros
        cots[i, pl.ds(7, cols, stride=8), :] = zeros
        for k in range(6):
            cots[i, pl.ds(k + 1, cols, stride=8), :] = cotf[pl.ds(2 * cols * k + i, cols, stride=2), :]

    group = TAPS * 8
    for end in (0, cols + 1):
        rows[pl.ds(end * group, group), :] = jnp.zeros((group, 256), BF)
        gp[pl.ds(end * 64, 64), :] = jnp.zeros((64, 256), BF)

    def spread(l, _):
        at = pl.multiple_of(l * 8, 8)
        taps = []
        for i in range(4):
            v = cs[i, pl.ds(at, 8), :]
            taps.append((shift_lanes(v, 1), v, shift_lanes(v, -1)))
        for i in range(2):
            block = [taps[i + a][b] for a in range(3) for b in range(3)]
            block.append(jnp.zeros((8, 128), F32))
            rows[pl.ds(pl.multiple_of((l + 1) * group, 16), group), pl.ds(i * 128, 128)] = jnp.concatenate(block, 0).astype(BF)
        return 0

    lax.fori_loop(0, cols, spread, 0, unroll=48)

    wf = wf_ref[...]
    wb = wb_ref[...]

    def forward(l, _):
        kind = jnp.where(l == 0, 0, jnp.where(l == cols - 1, 2, 1))
        window = rows[pl.ds(pl.multiple_of(l * group, 16), 3 * group), :]
        u = jnp.dot(wf, window, preferred_element_type=F32)
        u = u + bias_ref[pl.ds(pl.multiple_of(kind * 64, 64), 64), :]
        th = jnp.tanh(u)
        q = u * th
        g = (1.0 + u) + th * (1.0 - q)
        s = u + q
        at = pl.multiple_of(l * 8, 8)
        cot = jnp.concatenate([cots[0, pl.ds(at, 8), :], cots[1, pl.ds(at, 8), :]], 1)
        total = jnp.zeros((8, 256), F32)
        out = []
        for o in range(8):
            w = bias_ref[pl.ds(192 + o * 8, 8), :]
            total = total + w * s[o * 8:o * 8 + 8]
            out.append(g[o * 8:o * 8 + 8] * (cot * (0.5 * w)))
        gp[pl.ds(pl.multiple_of((l + 1) * 64, 64), 64), :] = jnp.concatenate(out, 0).astype(BF)
        sc[0, pl.ds(at, 8), :] = total[:, :128]
        sc[1, pl.ds(at, 8), :] = total[:, 128:]
        return 0

    lax.fori_loop(0, cols, forward, 0, unroll=96)

    def backward(m, _):
        window = gp[pl.ds(pl.multiple_of(m * 128, 128), 256), :]
        t = jnp.dot(wb, window, preferred_element_type=F32)
        at = pl.multiple_of(m * 8, 8)
        for io in range(4):
            part = []
            for b in range(3):
                pieces = []
                for a in range(3):
                    i = io - a
                    if 0 <= i < 2:
                        pieces.append(t[(b * 3 + a) * 8:(b * 3 + a) * 8 + 8, i * 128:(i + 1) * 128])
                part.append(functools.reduce(jnp.add, pieces))
            gs[io, pl.ds(at, 8), :] = shift_lanes(part[0], -1) + part[1] + shift_lanes(part[2], 1)
        return 0

    lax.fori_loop(0, cols // 2, backward, 0, unroll=48)

    for k in range(4):
        for i in range(2):
            cotf[pl.ds(2 * cols * k + i, cols, stride=2), :] = sc[i, pl.ds(k + 2, cols, stride=8), :]
    score_ref[...] = cotf[pl.ds(0, 8 * cols), :].astype(BF)
    for k in range(4):
        here = pl.ds(k * cols, cols)
        lo, mid_lo, mid_hi, hi = (gs[i, pl.ds(k, cols, stride=4), :] for i in range(4))
        g_ref[here, pl.ds(0, 128)] = mid_lo
        g_ref[here, pl.ds(128, 128)] = mid_hi
        far_out[here, :] = jnp.where(first, lo, hi).astype(BF)
        near_out[here, :] = jnp.where(first, hi, lo).astype(BF)


def conv(cols, scale, spot, weights, tgt, src, far, near, pair, next_, cot, halos):
    vmem = pl.BlockSpec(memory_space=pltpu.VMEM)
    smem = pl.BlockSpec(memory_space=pltpu.SMEM)
    n = 4 * cols
    return pl.pallas_call(
        functools.partial(conv_kernel, cols, scale),
        out_shape=(
            jax.ShapeDtypeStruct((8 * cols, 128), BF),
            jax.ShapeDtypeStruct((n, 256), F32),
            jax.ShapeDtypeStruct((n, 128), BF),
            jax.ShapeDtypeStruct((n, 128), BF),
        ),
        in_specs=[smem] + [vmem] * (10 + len(halos)),
        out_specs=(vmem,) * 4,
        scratch_shapes=[
            pltpu.VMEM((4, 8 * cols, 128), F32),
            pltpu.VMEM(((cols + 2) * TAPS * 8, 256), BF),
            pltpu.VMEM((12 * cols, 128), F32),
            pltpu.VMEM((2, 8 * cols, 128), F32),
            pltpu.VMEM(((cols + 2) * 64, 256), BF),
            pltpu.VMEM((2, 8 * cols, 128), F32),
            pltpu.VMEM((4, 4 * cols, 128), F32),
        ],
        compiler_params=pltpu.CompilerParams(vmem_limit_bytes=40 * 2**20),
        cost_estimate=pl.CostEstimate(flops=4 * 10**9, transcendentals=10**7, bytes_accessed=4 * 10**6),
    )(spot, *weights, tgt, src, far, near, pair, next_, cot, *halos)


def filters(w_src, b_src, w_tgt, b_tgt, w_out, first_row, total_rows):
    both = jnp.einsum(
        "opde,pab->odeab", w_tgt.astype(F32), w_src.astype(F32), precision=lax.Precision.HIGHEST
    )
    up = np.zeros((3, 8, 8), np.float32)
    for d in range(3):
        for m in range(1, 7):
            up[d, m, m + d - 1] = 1
    flat = jnp.pad(both.reshape(8, 3, 3, 9), ((0, 0), (0, 0), (0, 0), (0, TAPS - 9)))
    wf = (0.5 * jnp.einsum("odex,dmk->omexk", flat, up)).reshape(64, 3 * TAPS * 8).astype(BF)
    back = np.zeros((3, 4, 8), np.float32)
    side = np.zeros((3, 2, 4), np.float32)
    for d in range(3):
        for k in range(4):
            back[d, k, k + 3 - d] = 1
        for s in range(2):
            side[d, s, s + 2 - d] = 1
    spots = np.einsum("dkm,esl->desklm", back, side)
    wb = jnp.einsum("odeab,desklm->baskyom".replace("y", "l"), both, spots).reshape(72, 256).astype(BF)
    lift = jnp.einsum(
        "opde,p->ode", w_tgt.astype(F32), b_src, precision=lax.Precision.HIGHEST
    )
    row = first_row - 2 + jnp.arange(8)
    inside = ((row >= 0) & (row < total_rows)).astype(F32)
    edge = np.ones((3, 3), np.float32)
    edge[0, 0] = 0
    edge[2, 2] = 0
    along = jnp.einsum("ode,te->tod", lift, edge, precision=lax.Precision.HIGHEST)
    reach = jnp.einsum("dmk,k->md", up, inside, precision=lax.Precision.HIGHEST)
    bias = b_tgt[None, :, None] + jnp.einsum("tod,md->tom", along, reach, precision=lax.Precision.HIGHEST)
    bias = jnp.concatenate([(0.5 * bias).reshape(192), jnp.repeat(w_out, 8)])
    bias = jnp.broadcast_to(bias[:, None], (256, 256))
    return wf, wb, bias


SRC = ("z", "core")
TGT = ("y", "x", "zh")
SIZES = {"z": 4, "core": 2, "y": 4, "x": 4, "zh": 2}


def moved(x, move):
    n_src, n_tgt = lax.axis_size(SRC), lax.axis_size(TGT)
    pairs = []
    for a in range(n_src):
        for b in range(n_tgt):
            c, d = move(a, b)
            if 0 <= c < n_src and 0 <= d < n_tgt:
                pairs.append((a * n_tgt + b, c * n_tgt + d))
    return lax.ppermute(x, SRC + TGT, pairs)


def far_row(a, b):
    return (a + 1 if a % 2 else a - 1, b)


def near_row(a, b):
    return (a ^ 1, b)


def body(src_feat, tgt_feat, w_src, b_src, w_tgt, b_tgt, w_out, cotangent):
    rows_k, cols, rows_i, cols_j = cotangent.shape
    chans = tgt_feat.shape[2]
    scale = chans ** (-0.5)
    n_src, n_tgt = lax.axis_size(SRC), lax.axis_size(TGT)
    s, t, z, core, zh = (lax.axis_index(a) for a in (SRC, TGT, "z", "core", "zh"))
    first = core == 0
    block = chans // n_tgt
    pixels = rows_i * cols_j

    tgt_flat = tgt_feat.reshape(rows_k * cols, chans)
    cot = cotangent.reshape(rows_k * cols * rows_i, cols_j)
    width = chans // n_src
    hops = n_src // 2

    piece = src_feat.reshape(pixels, block).T
    line = cols * rows_i

    def edge(last, *extra):
        k = jnp.where(last, rows_k - 2, 0)
        part = lax.dynamic_slice(tgt_feat, (k, 0, s * width), (2, cols, width)).reshape(2 * cols, width)
        k = jnp.where(last, rows_k - 1, 0)
        return jnp.concatenate([part, lax.dynamic_slice(cot, (k * line, 0), (line, cols_j)), *extra], 0)

    even = zh == 0
    other = moved(piece, lambda a, b: (a, b ^ 1))
    pair_e, next_e = edge(even), edge(~even)
    next_e, other = lax.optimization_barrier((next_e, other))
    pair = moved(pair_e, lambda a, b: (a, b ^ 1))
    next_ = moved(next_e, lambda a, b: (a, b + 1 if b % 2 else b - 1))
    two = 2 * cols
    share = jnp.concatenate([pair[:two], next_[:two]], 0)
    shares = [share]
    for m in range(1, hops):
        shares.append(moved(share, lambda a, b, m=m: (a ^ (2 * m), b)))
    w_src, b_src, w_tgt, b_tgt, share = lax.optimization_barrier((w_src, b_src, w_tgt, b_tgt, share))
    weights = filters(w_src, b_src, w_tgt, b_tgt, w_out, t * rows_k, rows_k * n_tgt)

    both = jnp.where(even, jnp.concatenate([piece, other], 0), jnp.concatenate([other, piece], 0))
    plane = n_tgt // 2
    src_t = lax.all_to_all(
        jnp.broadcast_to(both[None], (plane, 2 * block, pixels)), ("y", "x"), 0, 0, tiled=True
    ).reshape(chans, pixels)
    src_t, *shares = lax.optimization_barrier((src_t, *shares))
    halos = []
    for mine in shares:
        halos += [mine, moved(mine, near_row)]
    low, high = src_t[:, :cols_j], src_t[:, cols_j:]
    near = moved(jnp.where(first, high, low), near_row)
    far = moved(jnp.where(first, low, high), far_row)

    spot = jnp.stack([z, core, zh]).astype(jnp.int32)
    score, g_own, to_far, to_near = conv(
        cols, scale, spot, weights, tgt_flat, src_t, far, near, pair, next_, cot, halos
    )
    from_near = moved(to_near, near_row)
    from_far = moved(to_far, far_row)
    g = jnp.concatenate(
        [
            g_own[:, :cols_j] + jnp.where(first, from_far, from_near).astype(F32),
            g_own[:, cols_j:] + jnp.where(first, from_near, from_far).astype(F32),
        ],
        1,
    ).astype(BF)

    cut = src_t.reshape(n_src, width, pixels)

    def blocks(side):
        return jnp.concatenate(
            [lax.dynamic_index_in_dim(cut, (z ^ m) * 2 + side, 0, False) for m in range(hops)], 0
        )

    over = (((1,), (1,)), ((), ()))
    other = lax.dot_general(g, blocks(1 - core), over, preferred_element_type=F32) * scale
    got = moved(other.astype(BF), near_row)
    mine = lax.dot_general(g, blocks(core), over, preferred_element_type=F32) * scale
    both = mine + got.astype(F32)
    total = both[:, :width]
    for m in range(1, hops):
        total = total + moved(
            both[:, m * width:(m + 1) * width].astype(BF), lambda a, b, m=m: (a ^ (2 * m), b)
        ).astype(F32)
    grad_tgt = total.reshape(rows_k, cols, width)

    part = lax.dot_general(tgt_flat, g, (((0,), (0,)), ((), ())), preferred_element_type=F32) * scale
    parts = lax.all_to_all(
        part.astype(BF).reshape(plane, 2 * block, pixels), ("y", "x"), 0, 0, tiled=True
    )
    halves = jnp.sum(parts.astype(F32), 0).reshape(2, block, pixels)
    keep = lax.dynamic_index_in_dim(halves, zh, 0, False)
    send = lax.dynamic_index_in_dim(halves, 1 - zh, 0, False)
    grad_src = keep + moved(send.astype(BF), lambda a, b: (a, b ^ 1)).astype(F32)
    return (score.reshape(cotangent.shape), grad_src.reshape(block, rows_i, cols_j), grad_tgt)


def solution(mesh):
    fine = jax.sharding.Mesh(mesh.devices.reshape(tuple(SIZES.values())), tuple(SIZES))
    placed = (
        P(SRC, None, TGT),
        P(TGT, None, None),
        P(),
        P(),
        P(),
        P(),
        P(),
        P(TGT, None, SRC, None),
    )
    return jax.shard_map(
        body,
        mesh=fine,
        in_specs=placed,
        out_specs=(P(TGT, None, SRC, None), P(TGT, SRC, None), P(TGT, None, SRC)),
        check_vma=False,
    )
```

```python
import functools

import jax
import jax.numpy as jnp
import numpy as np
from jax import lax
from jax.experimental import pallas as pl
from jax.experimental.pallas import tpu as pltpu
from jax.sharding import PartitionSpec as P

BF = jnp.bfloat16
F32 = jnp.float32
TAPS = 10


def shift_lanes(v, by):
    n = v.shape[1]
    lane = lax.broadcasted_iota(jnp.int32, v.shape, 1)
    edge = 0 if by == 1 else n - 1
    return jnp.where(lane == edge, 0.0, pltpu.roll(v, by % n, 1))


def conv_kernel(
    cols,
    scale, spot_ref, wf_ref, wb_ref, bias_ref, tgt_ref, src_ref, far_ref, near_ref, pair_ref, next_ref, cot_ref,
    *more,
):
    n_more = len(more) - 11
    halo_refs = more[:n_more]
    score_ref, g_ref, far_out, near_out, cs, rows, cotf, cots, gp, sc, gs = more[n_more:]
    hop, core = spot_ref[0], spot_ref[1]
    first = core == 0
    even = spot_ref[2] == 0

    def put(part, at, ks):
        part = (part * scale).astype(BF).astype(F32)
        for n, k in enumerate(ks):
            cs[at, pl.ds(k, cols, stride=8), :] = part[n * cols:(n + 1) * cols]

    def fill(product, ks):
        far, near = product(far_ref), product(near_ref)
        put(jnp.where(first, far, near), 0, ks)
        put(jnp.where(first, near, far), 3, ks)
        mid = product(src_ref)
        put(mid[:, :128], 1, ks)
        put(mid[:, 128:], 2, ks)

    def over_all(ref):
        return jnp.dot(tgt_ref[...], ref[...], preferred_element_type=F32)

    def over_pieces(ref):
        total = None
        for n, piece in enumerate(halo_refs):
            block = (hop ^ (n // 2)) * 2 + (core ^ (n % 2))
            part = jnp.dot(
                piece[...], ref[pl.ds(pl.multiple_of(block * 128, 128), 128), :], preferred_element_type=F32
            )
            total = part if total is None else total + part
        pair, next_ = total[:2 * cols], total[2 * cols:]
        return jnp.concatenate([jnp.where(even, next_, pair), jnp.where(even, pair, next_)], 0)

    fill(over_all, (2, 3, 4, 5))
    fill(over_pieces, (0, 1, 6, 7))
    zeros = jnp.zeros((cols, 128), F32)
    pair = pair_ref[pl.ds(2 * cols, 2 * cols), :].astype(F32)
    next_ = next_ref[pl.ds(0, 2 * cols), :].astype(F32)
    cotf[pl.ds(0, 2 * cols), :] = jnp.where(even, next_, pair)
    cotf[pl.ds(2 * cols, 8 * cols), :] = cot_ref[...].astype(F32)
    cotf[pl.ds(10 * cols, 2 * cols), :] = jnp.where(even, pair, next_)
    for i in range(2):
        cots[i, pl.ds(0, cols, stride=8), :] = zeros
        cots[i, pl.ds(7, cols, stride=8), :] = zeros
        for k in range(6):
            cots[i, pl.ds(k + 1, cols, stride=8), :] = cotf[pl.ds(2 * cols * k + i, cols, stride=2), :]

    group = TAPS * 8
    for end in (0, cols + 1):
        rows[pl.ds(end * group, group), :] = jnp.zeros((group, 256), BF)
        gp[pl.ds(end * 64, 64), :] = jnp.zeros((64, 256), BF)

    def spread(l, _):
        at = l * 8
        taps = []
        for i in range(4):
            v = cs[i, pl.ds(at, 8), :]
            taps.append((shift_lanes(v, 1), v, shift_lanes(v, -1)))
        for i in range(2):
            block = [taps[i + a][b] for a in range(3) for b in range(3)]
            block.append(jnp.zeros((8, 128), F32))
            rows[pl.ds((l + 1) * group, group), pl.ds(i * 128, 128)] = jnp.concatenate(block, 0).astype(BF)
        return 0


    wf = wf_ref[...]
    wb = wb_ref[...]

    def forward(l, _):
        kind = 0 if l == 0 else 2 if l == cols - 1 else 1
        window = rows[pl.ds(l * group, 3 * group), :]
        u = jnp.dot(wf, window, preferred_element_type=F32)
        u = u + bias_ref[pl.ds(kind * 64, 64), :]
        th = jnp.tanh(u)
        q = u * th
        g = (1.0 + u) + th * (1.0 - q)
        s = u + q
        at = l * 8
        cot = jnp.concatenate([cots[0, pl.ds(at, 8), :], cots[1, pl.ds(at, 8), :]], 1)
        total = jnp.zeros((8, 256), F32)
        out = []
        for o in range(8):
            w = bias_ref[pl.ds(192 + o * 8, 8), :]
            total = total + w * s[o * 8:o * 8 + 8]
            out.append(g[o * 8:o * 8 + 8] * (cot * (0.5 * w)))
        gp[pl.ds((l + 1) * 64, 64), :] = jnp.concatenate(out, 0).astype(BF)
        sc[0, pl.ds(at, 8), :] = total[:, :128]
        sc[1, pl.ds(at, 8), :] = total[:, 128:]
        return 0


    def backward(m, _):
        window = gp[pl.ds(m * 128, 256), :]
        t = jnp.dot(wb, window, preferred_element_type=F32)
        at = m * 8
        for io in range(4):
            part = []
            for b in range(3):
                pieces = []
                for a in range(3):
                    i = io - a
                    if 0 <= i < 2:
                        pieces.append(t[(b * 3 + a) * 8:(b * 3 + a) * 8 + 8, i * 128:(i + 1) * 128])
                part.append(functools.reduce(jnp.add, pieces))
            gs[io, pl.ds(at, 8), :] = shift_lanes(part[0], -1) + part[1] + shift_lanes(part[2], 1)
        return 0

    lag = 8
    for l in range(cols + 2 * lag):
        if l < cols:
            spread(l, 0)
        if lag <= l < cols + lag:
            forward(l - lag, 0)
        if l >= 2 * lag and l % 2 == 1:
            backward((l - 2 * lag) // 2, 0)

    for k in range(4):
        for i in range(2):
            cotf[pl.ds(2 * cols * k + i, cols, stride=2), :] = sc[i, pl.ds(k + 2, cols, stride=8), :]
    score_ref[...] = cotf[pl.ds(0, 8 * cols), :].astype(BF)
    for k in range(4):
        here = pl.ds(k * cols, cols)
        lo, mid_lo, mid_hi, hi = (gs[i, pl.ds(k, cols, stride=4), :] for i in range(4))
        g_ref[here, pl.ds(0, 128)] = mid_lo
        g_ref[here, pl.ds(128, 128)] = mid_hi
        far_out[here, :] = jnp.where(first, lo, hi).astype(BF)
        near_out[here, :] = jnp.where(first, hi, lo).astype(BF)


def conv(cols, scale, spot, weights, tgt, src, far, near, pair, next_, cot, halos):
    vmem = pl.BlockSpec(memory_space=pltpu.VMEM)
    smem = pl.BlockSpec(memory_space=pltpu.SMEM)
    n = 4 * cols
    return pl.pallas_call(
        functools.partial(conv_kernel, cols, scale),
        out_shape=(
            jax.ShapeDtypeStruct((8 * cols, 128), BF),
            jax.ShapeDtypeStruct((n, 256), F32),
            jax.ShapeDtypeStruct((n, 128), BF),
            jax.ShapeDtypeStruct((n, 128), BF),
        ),
        in_specs=[smem] + [pl.BlockSpec()] * 3 + [vmem] * (7 + len(halos)),
        out_specs=(vmem,) * 4,
        scratch_shapes=[
            pltpu.VMEM((4, 8 * cols, 128), F32),
            pltpu.VMEM(((cols + 2) * TAPS * 8, 256), BF),
            pltpu.VMEM((12 * cols, 128), F32),
            pltpu.VMEM((2, 8 * cols, 128), F32),
            pltpu.VMEM(((cols + 2) * 64, 256), BF),
            pltpu.VMEM((2, 8 * cols, 128), F32),
            pltpu.VMEM((4, 4 * cols, 128), F32),
        ],
        compiler_params=pltpu.CompilerParams(vmem_limit_bytes=40 * 2**20),
        cost_estimate=pl.CostEstimate(flops=4 * 10**9, transcendentals=10**7, bytes_accessed=4 * 10**6),
    )(spot, *weights, tgt, src, far, near, pair, next_, cot, *halos)


def tables():
    spread = np.zeros((9, 8, 256), np.float32)
    mask = np.zeros((9, 8, 256), np.float32)
    place = np.zeros((9, 8, 8, 256), np.float32)
    for d in range(3):
        for e in range(3):
            for m in range(1, 7):
                for x in range(9):
                    lane = (e * TAPS + x) * 8 + m + d - 1
                    spread[x, m, (e * TAPS + x) * 8:(e * TAPS + x) * 8 + 8] = 1
                    mask[d * 3 + e, m, lane] = 1
            for s in range(2):
                for k in range(4):
                    for o in range(8):
                        place[d * 3 + e, o, s * 4 + k, (s + 2 - e) * 64 + o * 8 + k + 3 - d] = 1
    return (
        jnp.asarray(spread.reshape(3, 3, 2048), BF),
        jnp.asarray(mask.reshape(9, 1, 2048), F32),
        jnp.asarray(place.reshape(9, 8, 2048), BF),
    )


def filters_kernel(
    total_rows,
    row_ref, wt_ref, ws_ref, b_src_ref, b_tgt_ref, w_out_ref, spread_ref, mask_ref, place_ref,
    wf_ref, wb_ref, bias_ref, forward, adjoint, bias,
):
    over_first = (((0,), (0,)), ((), ()))
    source = lanes = None
    for a in range(3):
        part = lax.dot_general(ws_ref[a], spread_ref[a], over_first, preferred_element_type=F32)
        source = part if source is None else source + part
    out = None
    for n in range(9):
        part = jnp.dot(wt_ref[n], (source * mask_ref[n]).astype(BF), preferred_element_type=F32)
        out = part if out is None else out + part
        part = lax.dot_general(wt_ref[n], place_ref[n], over_first, preferred_element_type=F32)
        lanes = part if lanes is None else lanes + part
    for m in range(8):
        for h in range(2):
            at = m * 256 + h * 128
            forward[h, pl.ds(m, 8, stride=8), :] = 0.5 * out[:, at:at + 128]
    wf_ref[...] = jnp.concatenate([forward[0], forward[1, :, :3 * TAPS * 8 - 128]], 1).astype(BF)
    lanes = lanes.astype(BF)
    for a in range(3):
        part = jnp.dot(ws_ref[a], lanes, preferred_element_type=F32)
        for c in range(8):
            for h in range(2):
                at = c * 256 + h * 128
                adjoint[h, pl.ds(a * 8 + c, 3, stride=24), :] = part[:, at:at + 128]
    wb_ref[...] = jnp.concatenate([adjoint[0], adjoint[1]], 1).astype(BF)

    def column(ref):
        v = jnp.broadcast_to(ref[...], (8, 8))
        same = lax.broadcasted_iota(jnp.int32, (8, 8), 0) == lax.broadcasted_iota(jnp.int32, (8, 8), 1)
        return jnp.sum(jnp.where(same, v, 0.0), 1, keepdims=True)

    b_tgt, w_out = column(b_tgt_ref), column(w_out_ref)
    lift = [jnp.sum(wt_ref[n].astype(F32) * b_src_ref[...], 1, keepdims=True) for n in range(9)]
    for kind in range(3):
        along = []
        for d in range(3):
            parts = [lift[d * 3 + e] for e in range(3) if (kind, e) not in ((0, 0), (2, 2))]
            along.append(functools.reduce(jnp.add, parts))
        for m in range(8):
            total = b_tgt
            for d in range(3):
                if 1 <= m <= 6:
                    row = row_ref[0] + (m + d - 3)
                    inside = jnp.logical_and(row >= 0, row < total_rows)
                    total = total + jnp.where(inside, along[d], 0.0)
            bias[pl.ds(kind * 64 + m, 8, stride=8), :] = jnp.broadcast_to(0.5 * total, (8, 128))
    for m in range(8):
        bias[pl.ds(192 + m, 8, stride=8), :] = jnp.broadcast_to(w_out, (8, 128))
    bias_ref[...] = jnp.concatenate([bias[...], bias[...]], 1)


def filters(w_src, b_src, w_tgt, b_tgt, w_out, first_row, total_rows):
    vmem = pl.BlockSpec(memory_space=pltpu.VMEM)
    smem = pl.BlockSpec(memory_space=pltpu.SMEM)
    return pl.pallas_call(
        functools.partial(filters_kernel, total_rows),
        out_shape=(
            jax.ShapeDtypeStruct((64, 3 * TAPS * 8), BF),
            jax.ShapeDtypeStruct((72, 256), BF),
            jax.ShapeDtypeStruct((256, 256), F32),
        ),
        in_specs=[smem] + [vmem] * 8,
        out_specs=(vmem,) * 3,
        scratch_shapes=[pltpu.VMEM((2, 64, 128), F32), pltpu.VMEM((2, 72, 128), F32), pltpu.VMEM((256, 128), F32)],
        cost_estimate=pl.CostEstimate(flops=10**9, transcendentals=0, bytes_accessed=10**6),
    )(
        first_row.astype(jnp.int32)[None],
        w_tgt.transpose(2, 3, 0, 1).reshape(9, 8, 8),
        w_src.transpose(1, 2, 0),
        b_src[None], b_tgt[None], w_out[None],
        *tables(),
    )


SRC = ("z", "core")
TGT = ("y", "x", "zh")
SIZES = {"z": 4, "core": 2, "y": 4, "x": 4, "zh": 2}


def moved(x, move):
    n_src, n_tgt = lax.axis_size(SRC), lax.axis_size(TGT)
    pairs = []
    for a in range(n_src):
        for b in range(n_tgt):
            c, d = move(a, b)
            if 0 <= c < n_src and 0 <= d < n_tgt:
                pairs.append((a * n_tgt + b, c * n_tgt + d))
    return lax.ppermute(x, SRC + TGT, pairs)


def far_row(a, b):
    return (a + 1 if a % 2 else a - 1, b)


def near_row(a, b):
    return (a ^ 1, b)


def body(src_feat, tgt_feat, w_src, b_src, w_tgt, b_tgt, w_out, cotangent):
    rows_k, cols, rows_i, cols_j = cotangent.shape
    chans = tgt_feat.shape[2]
    scale = chans ** (-0.5)
    n_src, n_tgt = lax.axis_size(SRC), lax.axis_size(TGT)
    s, t, z, core, zh = (lax.axis_index(a) for a in (SRC, TGT, "z", "core", "zh"))
    first = core == 0
    block = chans // n_tgt
    pixels = rows_i * cols_j

    tgt_flat = tgt_feat.reshape(rows_k * cols, chans)
    cot = cotangent.reshape(rows_k * cols * rows_i, cols_j)
    width = chans // n_src
    hops = n_src // 2

    piece = src_feat.reshape(pixels, block).T
    line = cols * rows_i

    def edge(last, swap):
        k = jnp.where(last, rows_k - 2, 0)
        part = lax.dynamic_slice(tgt_feat, (k, 0, s * width), (2, cols, width)).reshape(2 * cols, width)
        k = jnp.where(last, rows_k - 1, 0)
        parts = [part, lax.dynamic_slice(cot, (k * line, 0), (line, cols_j))]
        return jnp.concatenate(parts[::-1] if swap else parts, 0)

    even = zh == 0
    other = moved(piece, lambda a, b: (a, b ^ 1))
    pair_e, next_e = edge(even, False), edge(~even, True)
    next_e, other = lax.optimization_barrier((next_e, other))
    pair = moved(pair_e, lambda a, b: (a, b ^ 1))
    next_ = moved(next_e, lambda a, b: (a, b + 1 if b % 2 else b - 1))
    upper = lax.broadcasted_iota(jnp.int32, pair.shape, 0) < 2 * cols
    share = jnp.where(upper, pair, next_)
    shares = [share]
    for m in range(1, hops):
        shares.append(moved(share, lambda a, b, m=m: (a ^ (2 * m), b)))
    late = tgt_flat
    tgt_t = lax.optimization_barrier(late.T)
    weights = filters(w_src, b_src, w_tgt, b_tgt, w_out, t * rows_k, rows_k * n_tgt)

    both = jnp.where(even, jnp.concatenate([piece, other], 0), jnp.concatenate([other, piece], 0))
    plane = n_tgt // 2
    src_t = lax.all_to_all(
        jnp.broadcast_to(both[None], (plane, 2 * block, pixels)), ("y", "x"), 0, 0, tiled=True
    ).reshape(chans, pixels)
    halos = []
    for mine in shares:
        halos += [mine, moved(mine, near_row)]
    low, high = src_t[:, :cols_j], src_t[:, cols_j:]
    near = moved(jnp.where(first, high, low), near_row)
    far = moved(jnp.where(first, low, high), far_row)

    spot = jnp.stack([z, core, zh]).astype(jnp.int32)
    score, g_own, to_far, to_near = conv(
        cols, scale, spot, weights, tgt_flat, src_t, far, near, pair, next_, cot, halos
    )
    from_near = moved(to_near, near_row)
    from_far = moved(to_far, far_row)
    g = jnp.concatenate(
        [
            g_own[:, :cols_j] + jnp.where(first, from_far, from_near).astype(F32),
            g_own[:, cols_j:] + jnp.where(first, from_near, from_far).astype(F32),
        ],
        1,
    ).astype(BF)

    cut = src_t.reshape(n_src, width, pixels)

    def blocks(side):
        return jnp.concatenate(
            [lax.dynamic_index_in_dim(cut, (z ^ m) * 2 + side, 0, False) for m in range(hops)], 0
        )

    over = (((1,), (1,)), ((), ()))
    other = lax.dot_general(g, blocks(1 - core), over, preferred_element_type=F32) * scale
    got = moved(other.astype(BF), near_row)
    mine = lax.dot_general(g, blocks(core), over, preferred_element_type=F32) * scale
    both = mine + got.astype(F32)
    total = both[:, :width]
    for m in range(1, hops):
        total = total + moved(
            both[:, m * width:(m + 1) * width].astype(BF), lambda a, b, m=m: (a ^ (2 * m), b)
        ).astype(F32)
    grad_tgt = total.reshape(rows_k, cols, width)

    part = jnp.dot(tgt_t, g, preferred_element_type=F32) * scale
    parts = lax.all_to_all(
        part.astype(BF).reshape(plane, 2 * block, pixels), ("y", "x"), 0, 0, tiled=True
    )
    halves = jnp.sum(parts.astype(F32), 0).reshape(2, block, pixels)
    keep = lax.dynamic_index_in_dim(halves, zh, 0, False)
    send = lax.dynamic_index_in_dim(halves, 1 - zh, 0, False)
    grad_src = keep + moved(send.astype(BF), lambda a, b: (a, b ^ 1)).astype(F32)
    return (score.reshape(cotangent.shape), grad_src.reshape(block, rows_i, cols_j), grad_tgt)


def solution(mesh):
    fine = jax.sharding.Mesh(mesh.devices.reshape(tuple(SIZES.values())), tuple(SIZES))
    placed = (
        P(SRC, None, TGT),
        P(TGT, None, None),
        P(),
        P(),
        P(),
        P(),
        P(),
        P(TGT, None, SRC, None),
    )
    return jax.shard_map(
        body,
        mesh=fine,
        in_specs=placed,
        out_specs=(P(TGT, None, SRC, None), P(TGT, SRC, None), P(TGT, None, SRC)),
        check_vma=False,
    )
```

```python
import functools

import jax
import jax.numpy as jnp
import numpy as np
from jax import lax
from jax.experimental import pallas as pl
from jax.experimental.pallas import tpu as pltpu
from jax.sharding import PartitionSpec as P

BF = jnp.bfloat16
F32 = jnp.float32
TAPS = 10


def shift_lanes(v, by):
    n = v.shape[1]
    lane = lax.broadcasted_iota(jnp.int32, v.shape, 1)
    edge = 0 if by == 1 else n - 1
    return jnp.where(lane == edge, 0.0, pltpu.roll(v, by % n, 1))


def conv_kernel(
    cols,
    scale, spot_ref, wf_hbm, wb_hbm, bias_hbm, tgt_ref, src_ref, far_ref, near_ref, pair_ref, next_ref, cot_ref,
    *more,
):
    n_more = len(more) - 15
    halo_refs = more[:n_more]
    score_ref, g_ref, far_out, near_out, cs, rows, cotf, cots, gp, sc, gs, *filters_at = more[n_more:]
    wf_ref, wb_ref, bias_ref, arrived = filters_at
    fetched = [
        pltpu.make_async_copy(source, target, arrived.at[n])
        for n, (source, target) in enumerate(((wf_hbm, wf_ref), (wb_hbm, wb_ref), (bias_hbm, bias_ref)))
    ]
    for copy in fetched:
        copy.start()
    hop, core = spot_ref[0], spot_ref[1]
    first = core == 0
    even = spot_ref[2] == 0

    def put(part, at, ks):
        part = (part * scale).astype(BF).astype(F32)
        for n, k in enumerate(ks):
            cs[at, pl.ds(k, cols, stride=8), :] = part[n * cols:(n + 1) * cols]

    def fill(product, ks):
        far, near = product(far_ref), product(near_ref)
        put(jnp.where(first, far, near), 0, ks)
        put(jnp.where(first, near, far), 3, ks)
        mid = product(src_ref)
        put(mid[:, :128], 1, ks)
        put(mid[:, 128:], 2, ks)

    def over_all(ref):
        return jnp.dot(tgt_ref[...], ref[...], preferred_element_type=F32)

    def over_pieces(ref):
        total = None
        for n, piece in enumerate(halo_refs):
            block = (hop ^ (n // 2)) * 2 + (core ^ (n % 2))
            part = jnp.dot(
                piece[...], ref[pl.ds(pl.multiple_of(block * 128, 128), 128), :], preferred_element_type=F32
            )
            total = part if total is None else total + part
        pair, next_ = total[:2 * cols], total[2 * cols:]
        return jnp.concatenate([jnp.where(even, next_, pair), jnp.where(even, pair, next_)], 0)

    fill(over_all, (2, 3, 4, 5))
    fill(over_pieces, (0, 1, 6, 7))
    zeros = jnp.zeros((cols, 128), F32)
    pair = pair_ref[pl.ds(2 * cols, 2 * cols), :].astype(F32)
    next_ = next_ref[pl.ds(0, 2 * cols), :].astype(F32)
    cotf[pl.ds(0, 2 * cols), :] = jnp.where(even, next_, pair)
    cotf[pl.ds(2 * cols, 8 * cols), :] = cot_ref[...].astype(F32)
    cotf[pl.ds(10 * cols, 2 * cols), :] = jnp.where(even, pair, next_)
    for i in range(2):
        cots[i, pl.ds(0, cols, stride=8), :] = zeros
        cots[i, pl.ds(7, cols, stride=8), :] = zeros
        for k in range(6):
            cots[i, pl.ds(k + 1, cols, stride=8), :] = cotf[pl.ds(2 * cols * k + i, cols, stride=2), :]

    group = TAPS * 8
    for end in (0, cols + 1):
        rows[pl.ds(end * group, group), :] = jnp.zeros((group, 256), BF)
        gp[pl.ds(end * 64, 64), :] = jnp.zeros((64, 256), BF)

    def spread(l, _):
        at = l * 8
        taps = []
        for i in range(4):
            v = cs[i, pl.ds(at, 8), :]
            taps.append((shift_lanes(v, 1), v, shift_lanes(v, -1)))
        for i in range(2):
            block = [taps[i + a][b] for a in range(3) for b in range(3)]
            block.append(jnp.zeros((8, 128), F32))
            rows[pl.ds((l + 1) * group, group), pl.ds(i * 128, 128)] = jnp.concatenate(block, 0).astype(BF)
        return 0


    for copy in fetched:
        copy.wait()
    wf = wf_ref[...]
    wb = wb_ref[...]

    def forward(l, _):
        kind = 0 if l == 0 else 2 if l == cols - 1 else 1
        window = rows[pl.ds(l * group, 3 * group), :]
        u = jnp.dot(wf, window, preferred_element_type=F32)
        u = u + bias_ref[pl.ds(kind * 64, 64), :]
        th = jnp.tanh(u)
        q = u * th
        g = (1.0 + u) + th * (1.0 - q)
        s = u + q
        at = l * 8
        cot = jnp.concatenate([cots[0, pl.ds(at, 8), :], cots[1, pl.ds(at, 8), :]], 1)
        total = jnp.zeros((8, 256), F32)
        out = []
        for o in range(8):
            w = bias_ref[pl.ds(192 + o * 8, 8), :]
            total = total + w * s[o * 8:o * 8 + 8]
            out.append(g[o * 8:o * 8 + 8] * (cot * (0.5 * w)))
        gp[pl.ds((l + 1) * 64, 64), :] = jnp.concatenate(out, 0).astype(BF)
        sc[0, pl.ds(at, 8), :] = total[:, :128]
        sc[1, pl.ds(at, 8), :] = total[:, 128:]
        return 0


    def backward(m, _):
        window = gp[pl.ds(m * 128, 256), :]
        t = jnp.dot(wb, window, preferred_element_type=F32)
        at = m * 8
        for io in range(4):
            part = []
            for b in range(3):
                pieces = []
                for a in range(3):
                    i = io - a
                    if 0 <= i < 2:
                        pieces.append(t[(b * 3 + a) * 8:(b * 3 + a) * 8 + 8, i * 128:(i + 1) * 128])
                part.append(functools.reduce(jnp.add, pieces))
            gs[io, pl.ds(at, 8), :] = shift_lanes(part[0], -1) + part[1] + shift_lanes(part[2], 1)
        return 0

    lag = 8
    for l in range(cols + 2 * lag):
        if l < cols:
            spread(l, 0)
        if lag <= l < cols + lag:
            forward(l - lag, 0)
        if l >= 2 * lag and l % 2 == 1:
            backward((l - 2 * lag) // 2, 0)

    for k in range(4):
        for i in range(2):
            cotf[pl.ds(2 * cols * k + i, cols, stride=2), :] = sc[i, pl.ds(k + 2, cols, stride=8), :]
    score_ref[...] = cotf[pl.ds(0, 8 * cols), :].astype(BF)
    for k in range(4):
        here = pl.ds(k * cols, cols)
        lo, mid_lo, mid_hi, hi = (gs[i, pl.ds(k, cols, stride=4), :] for i in range(4))
        g_ref[here, pl.ds(0, 128)] = mid_lo
        g_ref[here, pl.ds(128, 128)] = mid_hi
        far_out[here, :] = jnp.where(first, lo, hi).astype(BF)
        near_out[here, :] = jnp.where(first, hi, lo).astype(BF)


def conv(cols, scale, spot, weights, tgt, src, far, near, pair, next_, cot, halos):
    vmem = pl.BlockSpec(memory_space=pltpu.VMEM)
    smem = pl.BlockSpec(memory_space=pltpu.SMEM)
    n = 4 * cols
    return pl.pallas_call(
        functools.partial(conv_kernel, cols, scale),
        out_shape=(
            jax.ShapeDtypeStruct((8 * cols, 128), BF),
            jax.ShapeDtypeStruct((n, 256), F32),
            jax.ShapeDtypeStruct((n, 128), BF),
            jax.ShapeDtypeStruct((n, 128), BF),
        ),
        in_specs=[smem] + [pl.BlockSpec(memory_space=pltpu.HBM)] * 3 + [vmem] * (7 + len(halos)),
        out_specs=(vmem,) * 4,
        scratch_shapes=[
            pltpu.VMEM((4, 8 * cols, 128), F32),
            pltpu.VMEM(((cols + 2) * TAPS * 8, 256), BF),
            pltpu.VMEM((12 * cols, 128), F32),
            pltpu.VMEM((2, 8 * cols, 128), F32),
            pltpu.VMEM(((cols + 2) * 64, 256), BF),
            pltpu.VMEM((2, 8 * cols, 128), F32),
            pltpu.VMEM((4, 4 * cols, 128), F32),
            *(pltpu.VMEM(w.shape, w.dtype) for w in weights),
            pltpu.SemaphoreType.DMA((3,)),
        ],
        compiler_params=pltpu.CompilerParams(vmem_limit_bytes=40 * 2**20),
        cost_estimate=pl.CostEstimate(flops=4 * 10**9, transcendentals=10**7, bytes_accessed=4 * 10**6),
    )(spot, *weights, tgt, src, far, near, pair, next_, cot, *halos)


def tables():
    spread = np.zeros((9, 8, 256), np.float32)
    mask = np.zeros((9, 8, 256), np.float32)
    place = np.zeros((9, 8, 8, 256), np.float32)
    for d in range(3):
        for e in range(3):
            for m in range(1, 7):
                for x in range(9):
                    lane = (e * TAPS + x) * 8 + m + d - 1
                    spread[x, m, (e * TAPS + x) * 8:(e * TAPS + x) * 8 + 8] = 1
                    mask[d * 3 + e, m, lane] = 1
            for s in range(2):
                for k in range(4):
                    for o in range(8):
                        place[d * 3 + e, o, s * 4 + k, (s + 2 - e) * 64 + o * 8 + k + 3 - d] = 1
    return (
        jnp.asarray(spread.reshape(3, 3, 2048), BF),
        jnp.asarray(mask.reshape(9, 1, 2048), F32),
        jnp.asarray(place.reshape(9, 8, 2048), BF),
    )


def filters_kernel(
    total_rows,
    row_ref, wt_ref, ws_ref, b_src_ref, b_tgt_ref, w_out_ref, spread_ref, mask_ref, place_ref,
    wf_ref, wb_ref, bias_ref, forward, adjoint, bias,
):
    over_first = (((0,), (0,)), ((), ()))
    source = lanes = None
    for a in range(3):
        part = lax.dot_general(ws_ref[a], spread_ref[a], over_first, preferred_element_type=F32)
        source = part if source is None else source + part
    out = None
    for n in range(9):
        part = jnp.dot(wt_ref[n], (source * mask_ref[n]).astype(BF), preferred_element_type=F32)
        out = part if out is None else out + part
        part = lax.dot_general(wt_ref[n], place_ref[n], over_first, preferred_element_type=F32)
        lanes = part if lanes is None else lanes + part
    for m in range(8):
        for h in range(2):
            at = m * 256 + h * 128
            forward[h, pl.ds(m, 8, stride=8), :] = 0.5 * out[:, at:at + 128]
    wf_ref[...] = jnp.concatenate([forward[0], forward[1, :, :3 * TAPS * 8 - 128]], 1).astype(BF)
    lanes = lanes.astype(BF)
    for a in range(3):
        part = jnp.dot(ws_ref[a], lanes, preferred_element_type=F32)
        for c in range(8):
            for h in range(2):
                at = c * 256 + h * 128
                adjoint[h, pl.ds(a * 8 + c, 3, stride=24), :] = part[:, at:at + 128]
    wb_ref[...] = jnp.concatenate([adjoint[0], adjoint[1]], 1).astype(BF)

    def column(ref):
        v = jnp.broadcast_to(ref[...], (8, 8))
        same = lax.broadcasted_iota(jnp.int32, (8, 8), 0) == lax.broadcasted_iota(jnp.int32, (8, 8), 1)
        return jnp.sum(jnp.where(same, v, 0.0), 1, keepdims=True)

    b_tgt, w_out = column(b_tgt_ref), column(w_out_ref)
    lift = [jnp.sum(wt_ref[n].astype(F32) * b_src_ref[...], 1, keepdims=True) for n in range(9)]
    for kind in range(3):
        along = []
        for d in range(3):
            parts = [lift[d * 3 + e] for e in range(3) if (kind, e) not in ((0, 0), (2, 2))]
            along.append(functools.reduce(jnp.add, parts))
        for m in range(8):
            total = b_tgt
            for d in range(3):
                if 1 <= m <= 6:
                    row = row_ref[0] + (m + d - 3)
                    inside = jnp.logical_and(row >= 0, row < total_rows)
                    total = total + jnp.where(inside, along[d], 0.0)
            bias[pl.ds(kind * 64 + m, 8, stride=8), :] = jnp.broadcast_to(0.5 * total, (8, 128))
    for m in range(8):
        bias[pl.ds(192 + m, 8, stride=8), :] = jnp.broadcast_to(w_out, (8, 128))
    bias_ref[...] = jnp.concatenate([bias[...], bias[...]], 1)


def filters(w_src, b_src, w_tgt, b_tgt, w_out, first_row, total_rows):
    vmem = pl.BlockSpec(memory_space=pltpu.VMEM)
    smem = pl.BlockSpec(memory_space=pltpu.SMEM)
    return pl.pallas_call(
        functools.partial(filters_kernel, total_rows),
        out_shape=(
            jax.ShapeDtypeStruct((64, 3 * TAPS * 8), BF),
            jax.ShapeDtypeStruct((72, 256), BF),
            jax.ShapeDtypeStruct((256, 256), F32),
        ),
        in_specs=[smem] + [vmem] * 8,
        out_specs=(vmem,) * 3,
        scratch_shapes=[pltpu.VMEM((2, 64, 128), F32), pltpu.VMEM((2, 72, 128), F32), pltpu.VMEM((256, 128), F32)],
        cost_estimate=pl.CostEstimate(flops=10**9, transcendentals=0, bytes_accessed=10**6),
    )(
        first_row.astype(jnp.int32)[None],
        w_tgt.transpose(2, 3, 0, 1).reshape(9, 8, 8),
        w_src.transpose(1, 2, 0),
        b_src[None], b_tgt[None], w_out[None],
        *tables(),
    )


SRC = ("z", "core")
TGT = ("y", "x", "zh")
SIZES = {"z": 4, "core": 2, "y": 4, "x": 4, "zh": 2}


def moved(x, move):
    n_src, n_tgt = lax.axis_size(SRC), lax.axis_size(TGT)
    pairs = []
    for a in range(n_src):
        for b in range(n_tgt):
            c, d = move(a, b)
            if 0 <= c < n_src and 0 <= d < n_tgt:
                pairs.append((a * n_tgt + b, c * n_tgt + d))
    return lax.ppermute(x, SRC + TGT, pairs)


def far_row(a, b):
    return (a + 1 if a % 2 else a - 1, b)


def near_row(a, b):
    return (a ^ 1, b)


def body(src_feat, tgt_feat, w_src, b_src, w_tgt, b_tgt, w_out, cotangent):
    rows_k, cols, rows_i, cols_j = cotangent.shape
    chans = tgt_feat.shape[2]
    scale = chans ** (-0.5)
    n_src, n_tgt = lax.axis_size(SRC), lax.axis_size(TGT)
    s, t, z, core, zh = (lax.axis_index(a) for a in (SRC, TGT, "z", "core", "zh"))
    first = core == 0
    block = chans // n_tgt
    pixels = rows_i * cols_j

    tgt_flat = tgt_feat.reshape(rows_k * cols, chans)
    cot = cotangent.reshape(rows_k * cols * rows_i, cols_j)
    width = chans // n_src
    hops = n_src // 2

    piece = src_feat.reshape(pixels, block).T
    line = cols * rows_i

    def edge(last, swap):
        k = jnp.where(last, rows_k - 2, 0)
        part = lax.dynamic_slice(tgt_feat, (k, 0, s * width), (2, cols, width)).reshape(2 * cols, width)
        k = jnp.where(last, rows_k - 1, 0)
        parts = [part, lax.dynamic_slice(cot, (k * line, 0), (line, cols_j))]
        return jnp.concatenate(parts[::-1] if swap else parts, 0)

    even = zh == 0
    other = moved(piece, lambda a, b: (a, b ^ 1))
    pair_e, next_e = edge(even, False), edge(~even, True)
    next_e, other = lax.optimization_barrier((next_e, other))
    pair = moved(pair_e, lambda a, b: (a, b ^ 1))
    next_ = moved(next_e, lambda a, b: (a, b + 1 if b % 2 else b - 1))
    upper = lax.broadcasted_iota(jnp.int32, pair.shape, 0) < 2 * cols
    share = jnp.where(upper, pair, next_)
    weights = filters(w_src, b_src, w_tgt, b_tgt, w_out, t * rows_k, rows_k * n_tgt)
    share, *weights = lax.optimization_barrier((share, *weights))
    shares = [share]
    for m in range(1, hops):
        shares.append(moved(share, lambda a, b, m=m: (a ^ (2 * m), b)))
    share, late = lax.optimization_barrier((share, tgt_flat))
    tgt_t = lax.optimization_barrier(late.T)

    both = jnp.where(even, jnp.concatenate([piece, other], 0), jnp.concatenate([other, piece], 0))
    plane = n_tgt // 2
    src_t = lax.all_to_all(
        jnp.broadcast_to(both[None], (plane, 2 * block, pixels)), ("y", "x"), 0, 0, tiled=True
    ).reshape(chans, pixels)
    src_t, *shares = lax.optimization_barrier((src_t, *shares))
    halos = []
    for mine in shares:
        halos += [mine, moved(mine, near_row)]
    low, high = src_t[:, :cols_j], src_t[:, cols_j:]
    near = moved(jnp.where(first, high, low), near_row)
    far = moved(jnp.where(first, low, high), far_row)

    spot = jnp.stack([z, core, zh]).astype(jnp.int32)
    score, g_own, to_far, to_near = conv(
        cols, scale, spot, weights, tgt_flat, src_t, far, near, pair, next_, cot, halos
    )
    from_near = moved(to_near, near_row)
    from_far = moved(to_far, far_row)
    g = jnp.concatenate(
        [
            g_own[:, :cols_j] + jnp.where(first, from_far, from_near).astype(F32),
            g_own[:, cols_j:] + jnp.where(first, from_near, from_far).astype(F32),
        ],
        1,
    ).astype(BF)

    cut = src_t.reshape(n_src, width, pixels)

    def blocks(side):
        return jnp.concatenate(
            [lax.dynamic_index_in_dim(cut, (z ^ m) * 2 + side, 0, False) for m in range(hops)], 0
        )

    over = (((1,), (1,)), ((), ()))
    other = lax.dot_general(g, blocks(1 - core), over, preferred_element_type=F32) * scale
    got = moved(other.astype(BF), near_row)
    mine = lax.dot_general(g, blocks(core), over, preferred_element_type=F32) * scale
    both = mine + got.astype(F32)
    total = both[:, :width]
    for m in range(1, hops):
        total = total + moved(
            both[:, m * width:(m + 1) * width].astype(BF), lambda a, b, m=m: (a ^ (2 * m), b)
        ).astype(F32)
    grad_tgt = total.reshape(rows_k, cols, width)

    part = jnp.dot(tgt_t, g, preferred_element_type=F32) * scale
    parts = lax.all_to_all(
        part.astype(BF).reshape(plane, 2 * block, pixels), ("y", "x"), 0, 0, tiled=True
    )
    halves = jnp.sum(parts.astype(F32), 0).reshape(2, block, pixels)
    keep = lax.dynamic_index_in_dim(halves, zh, 0, False)
    send = lax.dynamic_index_in_dim(halves, 1 - zh, 0, False)
    grad_src = keep + moved(send.astype(BF), lambda a, b: (a, b ^ 1)).astype(F32)
    return (score.reshape(cotangent.shape), grad_src.reshape(block, rows_i, cols_j), grad_tgt)


def solution(mesh):
    fine = jax.sharding.Mesh(mesh.devices.reshape(tuple(SIZES.values())), tuple(SIZES))
    placed = (
        P(SRC, None, TGT),
        P(TGT, None, None),
        P(),
        P(),
        P(),
        P(),
        P(),
        P(TGT, None, SRC, None),
    )
    return jax.shard_map(
        body,
        mesh=fine,
        in_specs=placed,
        out_specs=(P(TGT, None, SRC, None), P(TGT, SRC, None), P(TGT, None, SRC)),
        check_vma=False,
    )
```

```python
import functools

import jax
import jax.numpy as jnp
import numpy as np
from jax import lax
from jax.experimental import pallas as pl
from jax.experimental.pallas import tpu as pltpu
from jax.sharding import PartitionSpec as P

BF = jnp.bfloat16
F32 = jnp.float32
TAPS = 10


def shift_lanes(v, by):
    n = v.shape[1]
    lane = lax.broadcasted_iota(jnp.int32, v.shape, 1)
    edge = 0 if by == 1 else n - 1
    return jnp.where(lane == edge, 0.0, pltpu.roll(v, by % n, 1))


def conv_kernel(
    cols,
    scale, spot_ref, wf_hbm, wb_hbm, bias_hbm, tgt_ref, src_ref, far_ref, near_ref, pair_ref, next_ref, cot_ref,
    *more,
):
    n_more = len(more) - 15
    halo_refs = more[:n_more]
    score_ref, g_ref, far_out, near_out, cs, rows, cotf, cots, gp, sc, gs, *filters_at = more[n_more:]
    wf_ref, wb_ref, bias_ref, arrived = filters_at
    fetched = [
        pltpu.make_async_copy(source, target, arrived.at[n])
        for n, (source, target) in enumerate(((wf_hbm, wf_ref), (wb_hbm, wb_ref), (bias_hbm, bias_ref)))
    ]
    for copy in fetched:
        copy.start()
    hop, core = spot_ref[0], spot_ref[1]
    first = core == 0
    even = spot_ref[2] == 0

    def put(part, at, ks):
        part = (part * scale).astype(BF).astype(F32)
        for n, k in enumerate(ks):
            cs[at, pl.ds(k, cols, stride=8), :] = part[n * cols:(n + 1) * cols]

    def fill(product, ks):
        far, near = product(far_ref), product(near_ref)
        put(jnp.where(first, far, near), 0, ks)
        put(jnp.where(first, near, far), 3, ks)
        mid = product(src_ref)
        put(mid[:, :128], 1, ks)
        put(mid[:, 128:], 2, ks)

    def over_all(ref):
        return jnp.dot(tgt_ref[...], ref[...], preferred_element_type=F32)

    def over_pieces(ref):
        total = None
        for n, piece in enumerate(halo_refs):
            block = (hop ^ (n // 2)) * 2 + (core ^ (n % 2))
            part = jnp.dot(
                piece[...], ref[pl.ds(pl.multiple_of(block * 128, 128), 128), :], preferred_element_type=F32
            )
            total = part if total is None else total + part
        pair, next_ = total[:2 * cols], total[2 * cols:]
        return jnp.concatenate([jnp.where(even, next_, pair), jnp.where(even, pair, next_)], 0)

    fill(over_all, (2, 3, 4, 5))
    fill(over_pieces, (0, 1, 6, 7))
    zeros = jnp.zeros((cols, 128), F32)
    pair = pair_ref[pl.ds(2 * cols, 2 * cols), :].astype(F32)
    next_ = next_ref[pl.ds(0, 2 * cols), :].astype(F32)
    cotf[pl.ds(0, 2 * cols), :] = jnp.where(even, next_, pair)
    cotf[pl.ds(2 * cols, 8 * cols), :] = cot_ref[...].astype(F32)
    cotf[pl.ds(10 * cols, 2 * cols), :] = jnp.where(even, pair, next_)
    for i in range(2):
        cots[i, pl.ds(0, cols, stride=8), :] = zeros
        cots[i, pl.ds(7, cols, stride=8), :] = zeros
        for k in range(6):
            cots[i, pl.ds(k + 1, cols, stride=8), :] = cotf[pl.ds(2 * cols * k + i, cols, stride=2), :]

    group = TAPS * 8
    for end in (0, cols + 1):
        rows[pl.ds(end * group, group), :] = jnp.zeros((group, 256), BF)
        gp[pl.ds(end * 64, 64), :] = jnp.zeros((64, 256), BF)

    def spread(l, _):
        at = l * 8
        taps = []
        for i in range(4):
            v = cs[i, pl.ds(at, 8), :]
            taps.append((shift_lanes(v, 1), v, shift_lanes(v, -1)))
        for i in range(2):
            block = [taps[i + a][b] for a in range(3) for b in range(3)]
            block.append(jnp.zeros((8, 128), F32))
            rows[pl.ds((l + 1) * group, group), pl.ds(i * 128, 128)] = jnp.concatenate(block, 0).astype(BF)
        return 0


    for copy in fetched:
        copy.wait()
    wf = wf_ref[...]
    wb = wb_ref[...]

    def forward(l, _):
        kind = 0 if l == 0 else 2 if l == cols - 1 else 1
        window = rows[pl.ds(l * group, 3 * group), :]
        u = jnp.dot(wf, window, preferred_element_type=F32)
        u = u + bias_ref[pl.ds(kind * 64, 64), :]
        th = jnp.tanh(u)
        q = u * th
        g = (1.0 + u) + th * (1.0 - q)
        s = u + q
        at = l * 8
        cot = jnp.concatenate([cots[0, pl.ds(at, 8), :], cots[1, pl.ds(at, 8), :]], 1)
        total = jnp.zeros((8, 256), F32)
        out = []
        for o in range(8):
            w = bias_ref[pl.ds(192 + o * 8, 8), :]
            total = total + w * s[o * 8:o * 8 + 8]
            out.append(g[o * 8:o * 8 + 8] * (cot * (0.5 * w)))
        gp[pl.ds((l + 1) * 64, 64), :] = jnp.concatenate(out, 0).astype(BF)
        sc[0, pl.ds(at, 8), :] = total[:, :128]
        sc[1, pl.ds(at, 8), :] = total[:, 128:]
        return 0


    def backward(m, _):
        window = gp[pl.ds(m * 128, 256), :]
        t = jnp.dot(wb, window, preferred_element_type=F32)
        at = m * 8
        for io in range(4):
            part = []
            for b in range(3):
                pieces = []
                for a in range(3):
                    i = io - a
                    if 0 <= i < 2:
                        pieces.append(t[(b * 3 + a) * 8:(b * 3 + a) * 8 + 8, i * 128:(i + 1) * 128])
                part.append(functools.reduce(jnp.add, pieces))
            gs[io, pl.ds(at, 8), :] = shift_lanes(part[0], -1) + part[1] + shift_lanes(part[2], 1)
        return 0

    lag = 8
    for l in range(cols + 2 * lag):
        if l < cols:
            spread(l, 0)
        if lag <= l < cols + lag:
            forward(l - lag, 0)
        if l >= 2 * lag and l % 2 == 1:
            backward((l - 2 * lag) // 2, 0)

    for k in range(4):
        for i in range(2):
            cotf[pl.ds(2 * cols * k + i, cols, stride=2), :] = sc[i, pl.ds(k + 2, cols, stride=8), :]
    score_ref[...] = cotf[pl.ds(0, 8 * cols), :].astype(BF)
    for k in range(4):
        here = pl.ds(k * cols, cols)
        lo, mid_lo, mid_hi, hi = (gs[i, pl.ds(k, cols, stride=4), :] for i in range(4))
        g_ref[here, pl.ds(0, 128)] = mid_lo
        g_ref[here, pl.ds(128, 128)] = mid_hi
        far_out[here, :] = jnp.where(first, lo, hi).astype(BF)
        near_out[here, :] = jnp.where(first, hi, lo).astype(BF)


def conv(cols, scale, spot, weights, tgt, src, far, near, pair, next_, cot, halos):
    vmem = pl.BlockSpec(memory_space=pltpu.VMEM)
    smem = pl.BlockSpec(memory_space=pltpu.SMEM)
    n = 4 * cols
    return pl.pallas_call(
        functools.partial(conv_kernel, cols, scale),
        out_shape=(
            jax.ShapeDtypeStruct((8 * cols, 128), BF),
            jax.ShapeDtypeStruct((n, 256), F32),
            jax.ShapeDtypeStruct((n, 128), BF),
            jax.ShapeDtypeStruct((n, 128), BF),
        ),
        in_specs=[smem] + [pl.BlockSpec(memory_space=pltpu.HBM)] * 3 + [vmem] * (7 + len(halos)),
        out_specs=(vmem,) * 4,
        scratch_shapes=[
            pltpu.VMEM((4, 8 * cols, 128), F32),
            pltpu.VMEM(((cols + 2) * TAPS * 8, 256), BF),
            pltpu.VMEM((12 * cols, 128), F32),
            pltpu.VMEM((2, 8 * cols, 128), F32),
            pltpu.VMEM(((cols + 2) * 64, 256), BF),
            pltpu.VMEM((2, 8 * cols, 128), F32),
            pltpu.VMEM((4, 4 * cols, 128), F32),
            *(pltpu.VMEM(w.shape, w.dtype) for w in weights),
            pltpu.SemaphoreType.DMA((3,)),
        ],
        compiler_params=pltpu.CompilerParams(vmem_limit_bytes=40 * 2**20),
        cost_estimate=pl.CostEstimate(flops=4 * 10**9, transcendentals=10**7, bytes_accessed=4 * 10**6),
    )(spot, *weights, tgt, src, far, near, pair, next_, cot, *halos)


def tables():
    spread = np.zeros((9, 8, 256), np.float32)
    mask = np.zeros((9, 8, 256), np.float32)
    place = np.zeros((9, 8, 8, 256), np.float32)
    for d in range(3):
        for e in range(3):
            for m in range(1, 7):
                for x in range(9):
                    lane = (e * TAPS + x) * 8 + m + d - 1
                    spread[x, m, (e * TAPS + x) * 8:(e * TAPS + x) * 8 + 8] = 1
                    mask[d * 3 + e, m, lane] = 1
            for s in range(2):
                for k in range(4):
                    for o in range(8):
                        place[d * 3 + e, o, s * 4 + k, (s + 2 - e) * 64 + o * 8 + k + 3 - d] = 1
    return (
        jnp.asarray(spread.reshape(3, 3, 2048), BF),
        jnp.asarray(mask.reshape(9, 1, 2048), F32),
        jnp.asarray(place.reshape(9, 8, 2048), BF),
    )


def filters_kernel(
    total_rows,
    row_ref, wt_ref, ws_ref, b_src_ref, b_tgt_ref, w_out_ref, spread_ref, mask_ref, place_ref,
    wf_ref, wb_ref, bias_ref, forward, adjoint, bias,
):
    over_first = (((0,), (0,)), ((), ()))
    source = lanes = None
    for a in range(3):
        part = lax.dot_general(ws_ref[a], spread_ref[a], over_first, preferred_element_type=F32)
        source = part if source is None else source + part
    out = None
    for n in range(9):
        part = jnp.dot(wt_ref[n], (source * mask_ref[n]).astype(BF), preferred_element_type=F32)
        out = part if out is None else out + part
        part = lax.dot_general(wt_ref[n], place_ref[n], over_first, preferred_element_type=F32)
        lanes = part if lanes is None else lanes + part
    for m in range(8):
        for h in range(2):
            at = m * 256 + h * 128
            forward[h, pl.ds(m, 8, stride=8), :] = 0.5 * out[:, at:at + 128]
    wf_ref[...] = jnp.concatenate([forward[0], forward[1, :, :3 * TAPS * 8 - 128]], 1).astype(BF)
    lanes = lanes.astype(BF)
    for a in range(3):
        part = jnp.dot(ws_ref[a], lanes, preferred_element_type=F32)
        for c in range(8):
            for h in range(2):
                at = c * 256 + h * 128
                adjoint[h, pl.ds(a * 8 + c, 3, stride=24), :] = part[:, at:at + 128]
    wb_ref[...] = jnp.concatenate([adjoint[0], adjoint[1]], 1).astype(BF)

    def column(ref):
        v = jnp.broadcast_to(ref[...], (8, 8))
        same = lax.broadcasted_iota(jnp.int32, (8, 8), 0) == lax.broadcasted_iota(jnp.int32, (8, 8), 1)
        return jnp.sum(jnp.where(same, v, 0.0), 1, keepdims=True)

    b_tgt, w_out = column(b_tgt_ref), column(w_out_ref)
    lift = [jnp.sum(wt_ref[n].astype(F32) * b_src_ref[...], 1, keepdims=True) for n in range(9)]
    for kind in range(3):
        along = []
        for d in range(3):
            parts = [lift[d * 3 + e] for e in range(3) if (kind, e) not in ((0, 0), (2, 2))]
            along.append(functools.reduce(jnp.add, parts))
        for m in range(8):
            total = b_tgt
            for d in range(3):
                if 1 <= m <= 6:
                    row = row_ref[0] + (m + d - 3)
                    inside = jnp.logical_and(row >= 0, row < total_rows)
                    total = total + jnp.where(inside, along[d], 0.0)
            bias[pl.ds(kind * 64 + m, 8, stride=8), :] = jnp.broadcast_to(0.5 * total, (8, 128))
    for m in range(8):
        bias[pl.ds(192 + m, 8, stride=8), :] = jnp.broadcast_to(w_out, (8, 128))
    bias_ref[...] = jnp.concatenate([bias[...], bias[...]], 1)


def filters(w_src, b_src, w_tgt, b_tgt, w_out, first_row, total_rows):
    vmem = pl.BlockSpec(memory_space=pltpu.VMEM)
    smem = pl.BlockSpec(memory_space=pltpu.SMEM)
    return pl.pallas_call(
        functools.partial(filters_kernel, total_rows),
        out_shape=(
            jax.ShapeDtypeStruct((64, 3 * TAPS * 8), BF),
            jax.ShapeDtypeStruct((72, 256), BF),
            jax.ShapeDtypeStruct((256, 256), F32),
        ),
        in_specs=[smem] + [vmem] * 8,
        out_specs=(vmem,) * 3,
        scratch_shapes=[pltpu.VMEM((2, 64, 128), F32), pltpu.VMEM((2, 72, 128), F32), pltpu.VMEM((256, 128), F32)],
        cost_estimate=pl.CostEstimate(flops=4 * 10**9, transcendentals=0, bytes_accessed=10**6),
    )(
        first_row.astype(jnp.int32)[None],
        w_tgt.transpose(2, 3, 0, 1).reshape(9, 8, 8),
        w_src.transpose(1, 2, 0),
        b_src[None], b_tgt[None], w_out[None],
        *tables(),
    )


SRC = ("z", "core")
TGT = ("y", "x", "zh")
SIZES = {"z": 4, "core": 2, "y": 4, "x": 4, "zh": 2}


def moved(x, move):
    n_src, n_tgt = lax.axis_size(SRC), lax.axis_size(TGT)
    pairs = []
    for a in range(n_src):
        for b in range(n_tgt):
            c, d = move(a, b)
            if 0 <= c < n_src and 0 <= d < n_tgt:
                pairs.append((a * n_tgt + b, c * n_tgt + d))
    return lax.ppermute(x, SRC + TGT, pairs)


def far_row(a, b):
    return (a + 1 if a % 2 else a - 1, b)


def near_row(a, b):
    return (a ^ 1, b)


def body(src_feat, tgt_feat, w_src, b_src, w_tgt, b_tgt, w_out, cotangent):
    rows_k, cols, rows_i, cols_j = cotangent.shape
    chans = tgt_feat.shape[2]
    scale = chans ** (-0.5)
    n_src, n_tgt = lax.axis_size(SRC), lax.axis_size(TGT)
    s, t, z, core, zh = (lax.axis_index(a) for a in (SRC, TGT, "z", "core", "zh"))
    first = core == 0
    block = chans // n_tgt
    pixels = rows_i * cols_j

    tgt_flat = tgt_feat.reshape(rows_k * cols, chans)
    cot = cotangent.reshape(rows_k * cols * rows_i, cols_j)
    width = chans // n_src
    hops = n_src // 2

    piece = src_feat.reshape(pixels, block).T
    line = cols * rows_i

    def edge(last, swap):
        k = jnp.where(last, rows_k - 2, 0)
        part = lax.dynamic_slice(tgt_feat, (k, 0, s * width), (2, cols, width)).reshape(2 * cols, width)
        k = jnp.where(last, rows_k - 1, 0)
        parts = [part, lax.dynamic_slice(cot, (k * line, 0), (line, cols_j))]
        return jnp.concatenate(parts[::-1] if swap else parts, 0)

    even = zh == 0
    other = moved(piece, lambda a, b: (a, b ^ 1))
    pair_e, next_e = edge(even, False), edge(~even, True)
    next_e, other = lax.optimization_barrier((next_e, other))
    pair = moved(pair_e, lambda a, b: (a, b ^ 1))
    next_ = moved(next_e, lambda a, b: (a, b + 1 if b % 2 else b - 1))
    upper = lax.broadcasted_iota(jnp.int32, pair.shape, 0) < 2 * cols
    share = jnp.where(upper, pair, next_)
    w_src, b_src, w_tgt, b_tgt, share = lax.optimization_barrier((w_src, b_src, w_tgt, b_tgt, share))
    weights = filters(w_src, b_src, w_tgt, b_tgt, w_out, t * rows_k, rows_k * n_tgt)
    shares = [share]
    for m in range(1, hops):
        shares.append(moved(share, lambda a, b, m=m: (a ^ (2 * m), b)))
    share, late = lax.optimization_barrier((share, tgt_flat))
    tgt_t = lax.optimization_barrier(late.T)

    both = jnp.where(even, jnp.concatenate([piece, other], 0), jnp.concatenate([other, piece], 0))
    plane = n_tgt // 2
    src_t = lax.all_to_all(
        jnp.broadcast_to(both[None], (plane, 2 * block, pixels)), ("y", "x"), 0, 0, tiled=True
    ).reshape(chans, pixels)
    src_t, w0, w1, w2, *shares = lax.optimization_barrier((src_t, *weights, *shares))
    weights = (w0, w1, w2)
    halos = []
    for mine in shares:
        halos += [mine, moved(mine, near_row)]
    low, high = src_t[:, :cols_j], src_t[:, cols_j:]
    near = moved(jnp.where(first, high, low), near_row)
    far = moved(jnp.where(first, low, high), far_row)

    spot = jnp.stack([z, core, zh]).astype(jnp.int32)
    score, g_own, to_far, to_near = conv(
        cols, scale, spot, weights, tgt_flat, src_t, far, near, pair, next_, cot, halos
    )
    from_near = moved(to_near, near_row)
    from_far = moved(to_far, far_row)
    g = jnp.concatenate(
        [
            g_own[:, :cols_j] + jnp.where(first, from_far, from_near).astype(F32),
            g_own[:, cols_j:] + jnp.where(first, from_near, from_far).astype(F32),
        ],
        1,
    ).astype(BF)

    cut = src_t.reshape(n_src, width, pixels)

    def blocks(side):
        return jnp.concatenate(
            [lax.dynamic_index_in_dim(cut, (z ^ m) * 2 + side, 0, False) for m in range(hops)], 0
        )

    over = (((1,), (1,)), ((), ()))
    other = lax.dot_general(g, blocks(1 - core), over, preferred_element_type=F32) * scale
    got = moved(other.astype(BF), near_row)
    mine = lax.dot_general(g, blocks(core), over, preferred_element_type=F32) * scale
    both = mine + got.astype(F32)
    total = both[:, :width]
    for m in range(1, hops):
        total = total + moved(
            both[:, m * width:(m + 1) * width].astype(BF), lambda a, b, m=m: (a ^ (2 * m), b)
        ).astype(F32)
    grad_tgt = total.reshape(rows_k, cols, width)

    part = jnp.dot(tgt_t, g, preferred_element_type=F32) * scale
    parts = lax.all_to_all(
        part.astype(BF).reshape(plane, 2 * block, pixels), ("y", "x"), 0, 0, tiled=True
    )
    halves = jnp.sum(parts.astype(F32), 0).reshape(2, block, pixels)
    keep = lax.dynamic_index_in_dim(halves, zh, 0, False)
    send = lax.dynamic_index_in_dim(halves, 1 - zh, 0, False)
    grad_src = keep + moved(send.astype(BF), lambda a, b: (a, b ^ 1)).astype(F32)
    return (score.reshape(cotangent.shape), grad_src.reshape(block, rows_i, cols_j), grad_tgt)


def solution(mesh):
    fine = jax.sharding.Mesh(mesh.devices.reshape(tuple(SIZES.values())), tuple(SIZES))
    placed = (
        P(SRC, None, TGT),
        P(TGT, None, None),
        P(),
        P(),
        P(),
        P(),
        P(),
        P(TGT, None, SRC, None),
    )
    return jax.shard_map(
        body,
        mesh=fine,
        in_specs=placed,
        out_specs=(P(TGT, None, SRC, None), P(TGT, SRC, None), P(TGT, None, SRC)),
        check_vma=False,
    )
```

```python
import functools

import jax
import jax.numpy as jnp
import numpy as np
from jax import lax
from jax.experimental import pallas as pl
from jax.experimental.pallas import tpu as pltpu
from jax.sharding import PartitionSpec as P

BF = jnp.bfloat16
F32 = jnp.float32
TAPS = 10


def shift_lanes(v, by):
    n = v.shape[1]
    lane = lax.broadcasted_iota(jnp.int32, v.shape, 1)
    edge = 0 if by == 1 else n - 1
    return jnp.where(lane == edge, 0.0, pltpu.roll(v, by % n, 1))


def conv_kernel(
    cols,
    scale, spot_ref, wf_hbm, wb_hbm, bias_hbm, tgt_ref, src_ref, far_ref, near_ref, pair_ref, next_ref, cot_ref,
    *more,
):
    n_more = len(more) - 15
    halo_refs = more[:n_more]
    score_ref, g_ref, far_out, near_out, cs, rows, cotf, cots, gp, sc, gs, *filters_at = more[n_more:]
    wf_ref, wb_ref, bias_ref, arrived = filters_at
    fetched = [
        pltpu.make_async_copy(source, target, arrived.at[n])
        for n, (source, target) in enumerate(((wf_hbm, wf_ref), (wb_hbm, wb_ref), (bias_hbm, bias_ref)))
    ]
    for copy in fetched:
        copy.start()
    hop, core = spot_ref[0], spot_ref[1]
    first = core == 0
    even = spot_ref[2] == 0

    def put(part, at, ks):
        part = (part * scale).astype(BF).astype(F32)
        for n, k in enumerate(ks):
            cs[at, pl.ds(k, cols, stride=8), :] = part[n * cols:(n + 1) * cols]

    def fill(product, ks):
        far, near = product(far_ref), product(near_ref)
        put(jnp.where(first, far, near), 0, ks)
        put(jnp.where(first, near, far), 3, ks)
        mid = product(src_ref)
        put(mid[:, :128], 1, ks)
        put(mid[:, 128:], 2, ks)

    def over_all(ref):
        return jnp.dot(tgt_ref[...], ref[...], preferred_element_type=F32)

    def over_pieces(ref):
        total = None
        for n, piece in enumerate(halo_refs):
            block = (hop ^ (n // 2)) * 2 + (core ^ (n % 2))
            part = jnp.dot(
                piece[...], ref[pl.ds(pl.multiple_of(block * 128, 128), 128), :], preferred_element_type=F32
            )
            total = part if total is None else total + part
        pair, next_ = total[:2 * cols], total[2 * cols:]
        return jnp.concatenate([jnp.where(even, next_, pair), jnp.where(even, pair, next_)], 0)

    fill(over_all, (2, 3, 4, 5))
    fill(over_pieces, (0, 1, 6, 7))
    zeros = jnp.zeros((cols, 128), F32)
    pair = pair_ref[pl.ds(2 * cols, 2 * cols), :].astype(F32)
    next_ = next_ref[pl.ds(0, 2 * cols), :].astype(F32)
    cotf[pl.ds(0, 2 * cols), :] = jnp.where(even, next_, pair)
    cotf[pl.ds(2 * cols, 8 * cols), :] = cot_ref[...].astype(F32)
    cotf[pl.ds(10 * cols, 2 * cols), :] = jnp.where(even, pair, next_)
    for i in range(2):
        cots[i, pl.ds(0, cols, stride=8), :] = zeros
        cots[i, pl.ds(7, cols, stride=8), :] = zeros
        for k in range(6):
            cots[i, pl.ds(k + 1, cols, stride=8), :] = cotf[pl.ds(2 * cols * k + i, cols, stride=2), :]

    group = TAPS * 8
    for end in (0, cols + 1):
        rows[pl.ds(end * group, group), :] = jnp.zeros((group, 256), BF)
        gp[pl.ds(end * 64, 64), :] = jnp.zeros((64, 256), BF)

    def spread(l, _):
        at = l * 8
        taps = []
        for i in range(4):
            v = cs[i, pl.ds(at, 8), :]
            taps.append((shift_lanes(v, 1), v, shift_lanes(v, -1)))
        for i in range(2):
            block = [taps[i + a][b] for a in range(3) for b in range(3)]
            block.append(jnp.zeros((8, 128), F32))
            rows[pl.ds((l + 1) * group, group), pl.ds(i * 128, 128)] = jnp.concatenate(block, 0).astype(BF)
        return 0


    for copy in fetched:
        copy.wait()
    wf = wf_ref[...]
    wb = wb_ref[...]

    def forward(l, _):
        kind = 0 if l == 0 else 2 if l == cols - 1 else 1
        window = rows[pl.ds(l * group, 3 * group), :]
        u = jnp.dot(wf, window, preferred_element_type=F32)
        b = bias_ref[pl.ds(kind * 64, 64), :]
        u = u + jnp.concatenate([b, b], 1)
        th = jnp.tanh(u)
        q = u * th
        g = (1.0 + u) + th * (1.0 - q)
        s = u + q
        at = l * 8
        cot = jnp.concatenate([cots[0, pl.ds(at, 8), :], cots[1, pl.ds(at, 8), :]], 1)
        total = jnp.zeros((8, 256), F32)
        out = []
        for o in range(8):
            w = bias_ref[pl.ds(192 + o * 8, 8), :]
            w = jnp.concatenate([w, w], 1)
            total = total + w * s[o * 8:o * 8 + 8]
            out.append(g[o * 8:o * 8 + 8] * (cot * (0.5 * w)))
        gp[pl.ds((l + 1) * 64, 64), :] = jnp.concatenate(out, 0).astype(BF)
        sc[0, pl.ds(at, 8), :] = total[:, :128]
        sc[1, pl.ds(at, 8), :] = total[:, 128:]
        return 0


    def backward(m, _):
        window = gp[pl.ds(m * 128, 256), :]
        t = jnp.dot(wb, window, preferred_element_type=F32)
        at = m * 8
        for io in range(4):
            part = []
            for b in range(3):
                pieces = []
                for a in range(3):
                    i = io - a
                    if 0 <= i < 2:
                        pieces.append(t[(b * 3 + a) * 8:(b * 3 + a) * 8 + 8, i * 128:(i + 1) * 128])
                part.append(functools.reduce(jnp.add, pieces))
            gs[io, pl.ds(at, 8), :] = shift_lanes(part[0], -1) + part[1] + shift_lanes(part[2], 1)
        return 0

    lag = 8
    for l in range(cols + 2 * lag):
        if l < cols:
            spread(l, 0)
        if lag <= l < cols + lag:
            forward(l - lag, 0)
        if l >= 2 * lag and l % 2 == 1:
            backward((l - 2 * lag) // 2, 0)

    for k in range(4):
        for i in range(2):
            cotf[pl.ds(2 * cols * k + i, cols, stride=2), :] = sc[i, pl.ds(k + 2, cols, stride=8), :]
    score_ref[...] = cotf[pl.ds(0, 8 * cols), :].astype(BF)
    for k in range(4):
        here = pl.ds(k * cols, cols)
        lo, mid_lo, mid_hi, hi = (gs[i, pl.ds(k, cols, stride=4), :] for i in range(4))
        g_ref[here, pl.ds(0, 128)] = mid_lo
        g_ref[here, pl.ds(128, 128)] = mid_hi
        far_out[here, :] = jnp.where(first, lo, hi).astype(BF)
        near_out[here, :] = jnp.where(first, hi, lo).astype(BF)


def conv(cols, scale, spot, weights, tgt, src, far, near, pair, next_, cot, halos):
    vmem = pl.BlockSpec(memory_space=pltpu.VMEM)
    smem = pl.BlockSpec(memory_space=pltpu.SMEM)
    n = 4 * cols
    return pl.pallas_call(
        functools.partial(conv_kernel, cols, scale),
        out_shape=(
            jax.ShapeDtypeStruct((8 * cols, 128), BF),
            jax.ShapeDtypeStruct((n, 256), F32),
            jax.ShapeDtypeStruct((n, 128), BF),
            jax.ShapeDtypeStruct((n, 128), BF),
        ),
        in_specs=[smem] + [pl.BlockSpec(memory_space=pltpu.HBM)] * 3 + [vmem] * (7 + len(halos)),
        out_specs=(vmem,) * 4,
        scratch_shapes=[
            pltpu.VMEM((4, 8 * cols, 128), F32),
            pltpu.VMEM(((cols + 2) * TAPS * 8, 256), BF),
            pltpu.VMEM((12 * cols, 128), F32),
            pltpu.VMEM((2, 8 * cols, 128), F32),
            pltpu.VMEM(((cols + 2) * 64, 256), BF),
            pltpu.VMEM((2, 8 * cols, 128), F32),
            pltpu.VMEM((4, 4 * cols, 128), F32),
            *(pltpu.VMEM(w.shape, w.dtype) for w in weights),
            pltpu.SemaphoreType.DMA((3,)),
        ],
        compiler_params=pltpu.CompilerParams(vmem_limit_bytes=40 * 2**20),
        cost_estimate=pl.CostEstimate(flops=4 * 10**9, transcendentals=10**7, bytes_accessed=4 * 10**6),
    )(spot, *weights, tgt, src, far, near, pair, next_, cot, *halos)


def tables():
    spread = np.zeros((9, 8, 256), np.float32)
    mask = np.zeros((9, 8, 256), np.float32)
    place = np.zeros((9, 8, 8, 256), np.float32)
    for d in range(3):
        for e in range(3):
            for m in range(1, 7):
                for x in range(9):
                    lane = (e * TAPS + x) * 8 + m + d - 1
                    spread[x, m, (e * TAPS + x) * 8:(e * TAPS + x) * 8 + 8] = 1
                    mask[d * 3 + e, m, lane] = 1
            for s in range(2):
                for k in range(4):
                    for o in range(8):
                        place[d * 3 + e, o, s * 4 + k, (s + 2 - e) * 64 + o * 8 + k + 3 - d] = 1
    return (
        jnp.asarray(spread.reshape(3, 3, 2048), BF),
        jnp.asarray(mask.reshape(9, 1, 2048), F32),
        jnp.asarray(place.reshape(9, 8, 2048), BF),
    )


def filters_kernel(
    total_rows,
    row_ref, wt_ref, ws_ref, b_src_ref, b_tgt_ref, w_out_ref, spread_ref, mask_ref, place_ref,
    wf_ref, wb_ref, bias_ref, forward, adjoint,
):
    over_first = (((0,), (0,)), ((), ()))
    source = lanes = None
    for a in range(3):
        part = lax.dot_general(ws_ref[a], spread_ref[a], over_first, preferred_element_type=F32)
        source = part if source is None else source + part
    out = None
    for n in range(9):
        part = jnp.dot(wt_ref[n], (source * mask_ref[n]).astype(BF), preferred_element_type=F32)
        out = part if out is None else out + part
        part = lax.dot_general(wt_ref[n], place_ref[n], over_first, preferred_element_type=F32)
        lanes = part if lanes is None else lanes + part
    for m in range(8):
        for h in range(2):
            at = m * 256 + h * 128
            forward[h, pl.ds(m, 8, stride=8), :] = 0.5 * out[:, at:at + 128]
    wf_ref[...] = jnp.concatenate([forward[0], forward[1, :, :3 * TAPS * 8 - 128]], 1).astype(BF)
    lanes = lanes.astype(BF)
    for a in range(3):
        part = jnp.dot(ws_ref[a], lanes, preferred_element_type=F32)
        for c in range(8):
            for h in range(2):
                at = c * 256 + h * 128
                adjoint[h, pl.ds(a * 8 + c, 3, stride=24), :] = part[:, at:at + 128]
    wb_ref[...] = jnp.concatenate([adjoint[0], adjoint[1]], 1).astype(BF)

    def column(ref):
        v = jnp.broadcast_to(ref[...], (8, 8))
        same = lax.broadcasted_iota(jnp.int32, (8, 8), 0) == lax.broadcasted_iota(jnp.int32, (8, 8), 1)
        return jnp.sum(jnp.where(same, v, 0.0), 1, keepdims=True)

    b_tgt, w_out = column(b_tgt_ref), column(w_out_ref)
    lift = [jnp.sum(wt_ref[n].astype(F32) * b_src_ref[...], 1, keepdims=True) for n in range(9)]
    for kind in range(3):
        along = []
        for d in range(3):
            parts = [lift[d * 3 + e] for e in range(3) if (kind, e) not in ((0, 0), (2, 2))]
            along.append(functools.reduce(jnp.add, parts))
        for m in range(8):
            total = b_tgt
            for d in range(3):
                if 1 <= m <= 6:
                    row = row_ref[0] + (m + d - 3)
                    inside = jnp.logical_and(row >= 0, row < total_rows)
                    total = total + jnp.where(inside, along[d], 0.0)
            bias_ref[pl.ds(kind * 64 + m, 8, stride=8), :] = jnp.broadcast_to(0.5 * total, (8, 128))
    for m in range(8):
        bias_ref[pl.ds(192 + m, 8, stride=8), :] = jnp.broadcast_to(w_out, (8, 128))


def filters(w_src, b_src, w_tgt, b_tgt, w_out, first_row, total_rows):
    vmem = pl.BlockSpec(memory_space=pltpu.VMEM)
    smem = pl.BlockSpec(memory_space=pltpu.SMEM)
    return pl.pallas_call(
        functools.partial(filters_kernel, total_rows),
        out_shape=(
            jax.ShapeDtypeStruct((64, 3 * TAPS * 8), BF),
            jax.ShapeDtypeStruct((72, 256), BF),
            jax.ShapeDtypeStruct((256, 128), F32),
        ),
        in_specs=[smem] + [vmem] * 8,
        out_specs=(vmem,) * 3,
        scratch_shapes=[pltpu.VMEM((2, 64, 128), F32), pltpu.VMEM((2, 72, 128), F32)],
        cost_estimate=pl.CostEstimate(flops=4 * 10**9, transcendentals=0, bytes_accessed=10**6),
    )(
        first_row.astype(jnp.int32)[None],
        w_tgt.transpose(2, 3, 0, 1).reshape(9, 8, 8),
        w_src.transpose(1, 2, 0),
        b_src[None], b_tgt[None], w_out[None],
        *tables(),
    )


SRC = ("z", "core")
TGT = ("y", "x", "zh")
SIZES = {"z": 4, "core": 2, "y": 4, "x": 4, "zh": 2}


def moved(x, move):
    n_src, n_tgt = lax.axis_size(SRC), lax.axis_size(TGT)
    pairs = []
    for a in range(n_src):
        for b in range(n_tgt):
            c, d = move(a, b)
            if 0 <= c < n_src and 0 <= d < n_tgt:
                pairs.append((a * n_tgt + b, c * n_tgt + d))
    return lax.ppermute(x, SRC + TGT, pairs)


def far_row(a, b):
    return (a + 1 if a % 2 else a - 1, b)


def near_row(a, b):
    return (a ^ 1, b)


def body(src_feat, tgt_feat, w_src, b_src, w_tgt, b_tgt, w_out, cotangent):
    rows_k, cols, rows_i, cols_j = cotangent.shape
    chans = tgt_feat.shape[2]
    scale = chans ** (-0.5)
    n_src, n_tgt = lax.axis_size(SRC), lax.axis_size(TGT)
    s, t, z, core, zh = (lax.axis_index(a) for a in (SRC, TGT, "z", "core", "zh"))
    first = core == 0
    block = chans // n_tgt
    pixels = rows_i * cols_j

    tgt_flat = tgt_feat.reshape(rows_k * cols, chans)
    cot = cotangent.reshape(rows_k * cols * rows_i, cols_j)
    width = chans // n_src
    hops = n_src // 2

    piece = src_feat.reshape(pixels, block).T
    line = cols * rows_i

    def edge(last, swap):
        k = jnp.where(last, rows_k - 2, 0)
        part = lax.dynamic_slice(tgt_feat, (k, 0, s * width), (2, cols, width)).reshape(2 * cols, width)
        k = jnp.where(last, rows_k - 1, 0)
        parts = [part, lax.dynamic_slice(cot, (k * line, 0), (line, cols_j))]
        return jnp.concatenate(parts[::-1] if swap else parts, 0)

    even = zh == 0
    other = moved(piece, lambda a, b: (a, b ^ 1))
    pair_e, next_e = edge(even, False), edge(~even, True)
    next_e, other = lax.optimization_barrier((next_e, other))
    pair = moved(pair_e, lambda a, b: (a, b ^ 1))
    next_ = moved(next_e, lambda a, b: (a, b + 1 if b % 2 else b - 1))
    upper = lax.broadcasted_iota(jnp.int32, pair.shape, 0) < 2 * cols
    share = jnp.where(upper, pair, next_)
    w_src, b_src, w_tgt, b_tgt, share = lax.optimization_barrier((w_src, b_src, w_tgt, b_tgt, share))
    weights = filters(w_src, b_src, w_tgt, b_tgt, w_out, t * rows_k, rows_k * n_tgt)
    shares = [share]
    for m in range(1, hops):
        shares.append(moved(share, lambda a, b, m=m: (a ^ (2 * m), b)))
    share, late = lax.optimization_barrier((share, tgt_flat))
    tgt_t = lax.optimization_barrier(late.T)

    both = jnp.where(even, jnp.concatenate([piece, other], 0), jnp.concatenate([other, piece], 0))
    plane = n_tgt // 2
    src_t = lax.all_to_all(
        jnp.broadcast_to(both[None], (plane, 2 * block, pixels)), ("y", "x"), 0, 0, tiled=True
    ).reshape(chans, pixels)
    src_t, w0, w1, w2, *shares = lax.optimization_barrier((src_t, *weights, *shares))
    weights = (w0, w1, w2)
    halos = []
    for mine in shares:
        halos += [mine, moved(mine, near_row)]
    low, high = src_t[:, :cols_j], src_t[:, cols_j:]
    near = moved(jnp.where(first, high, low), near_row)
    far = moved(jnp.where(first, low, high), far_row)

    spot = jnp.stack([z, core, zh]).astype(jnp.int32)
    score, g_own, to_far, to_near = conv(
        cols, scale, spot, weights, tgt_flat, src_t, far, near, pair, next_, cot, halos
    )
    from_near = moved(to_near, near_row)
    from_far = moved(to_far, far_row)
    g = jnp.concatenate(
        [
            g_own[:, :cols_j] + jnp.where(first, from_far, from_near).astype(F32),
            g_own[:, cols_j:] + jnp.where(first, from_near, from_far).astype(F32),
        ],
        1,
    ).astype(BF)

    cut = src_t.reshape(n_src, width, pixels)

    def blocks(side):
        return jnp.concatenate(
            [lax.dynamic_index_in_dim(cut, (z ^ m) * 2 + side, 0, False) for m in range(hops)], 0
        )

    over = (((1,), (1,)), ((), ()))
    other = lax.dot_general(g, blocks(1 - core), over, preferred_element_type=F32) * scale
    got = moved(other.astype(BF), near_row)
    mine = lax.dot_general(g, blocks(core), over, preferred_element_type=F32) * scale
    both = mine + got.astype(F32)
    total = both[:, :width]
    for m in range(1, hops):
        total = total + moved(
            both[:, m * width:(m + 1) * width].astype(BF), lambda a, b, m=m: (a ^ (2 * m), b)
        ).astype(F32)
    grad_tgt = total.reshape(rows_k, cols, width)

    part = jnp.dot(tgt_t, g, preferred_element_type=F32) * scale
    parts = lax.all_to_all(
        part.astype(BF).reshape(plane, 2 * block, pixels), ("y", "x"), 0, 0, tiled=True
    )
    halves = jnp.sum(parts.astype(F32), 0).reshape(2, block, pixels)
    keep = lax.dynamic_index_in_dim(halves, zh, 0, False)
    send = lax.dynamic_index_in_dim(halves, 1 - zh, 0, False)
    grad_src = keep + moved(send.astype(BF), lambda a, b: (a, b ^ 1)).astype(F32)
    return (score.reshape(cotangent.shape), grad_src.reshape(block, rows_i, cols_j), grad_tgt)


def solution(mesh):
    fine = jax.sharding.Mesh(mesh.devices.reshape(tuple(SIZES.values())), tuple(SIZES))
    placed = (
        P(SRC, None, TGT),
        P(TGT, None, None),
        P(),
        P(),
        P(),
        P(),
        P(),
        P(TGT, None, SRC, None),
    )
    return jax.shard_map(
        body,
        mesh=fine,
        in_specs=placed,
        out_specs=(P(TGT, None, SRC, None), P(TGT, SRC, None), P(TGT, None, SRC)),
        check_vma=False,
    )
```

```python
import functools

import jax
import jax.numpy as jnp
import numpy as np
from jax import lax
from jax.experimental import pallas as pl
from jax.experimental.pallas import tpu as pltpu
from jax.sharding import PartitionSpec as P

BF = jnp.bfloat16
F32 = jnp.float32
TAPS = 10


def shift_lanes(v, by):
    n = v.shape[1]
    lane = lax.broadcasted_iota(jnp.int32, v.shape, 1)
    edge = 0 if by == 1 else n - 1
    return jnp.where(lane == edge, 0.0, pltpu.roll(v, by % n, 1))


def conv_kernel(
    cols,
    scale, spot_ref, wf_hbm, wb_hbm, bias_hbm, tgt_ref, src_ref, far_ref, near_ref, pair_ref, next_ref, cot_ref,
    *more,
):
    n_more = len(more) - 15
    halo_refs = more[:n_more]
    score_ref, g_ref, far_out, near_out, cs, rows, cotf, cots, gp, sc, gs, *filters_at = more[n_more:]
    wf_ref, wb_ref, bias_ref, arrived = filters_at
    fetched = [
        pltpu.make_async_copy(source, target, arrived.at[n])
        for n, (source, target) in enumerate(((wf_hbm, wf_ref), (wb_hbm, wb_ref), (bias_hbm, bias_ref)))
    ]
    for copy in fetched:
        copy.start()
    hop, core = spot_ref[0], spot_ref[1]
    first = core == 0
    even = spot_ref[2] == 0

    def put(part, at, ks):
        part = (part * scale).astype(BF).astype(F32)
        for n, k in enumerate(ks):
            cs[at, pl.ds(k, cols, stride=8), :] = part[n * cols:(n + 1) * cols]

    def fill(product, ks):
        far, near = product(far_ref), product(near_ref)
        put(jnp.where(first, far, near), 0, ks)
        put(jnp.where(first, near, far), 3, ks)
        mid = product(src_ref)
        put(mid[:, :128], 1, ks)
        put(mid[:, 128:], 2, ks)

    def over_all(ref):
        return jnp.dot(tgt_ref[...], ref[...], preferred_element_type=F32)

    def over_pieces(ref):
        total = None
        for n, piece in enumerate(halo_refs):
            block = (hop ^ (n // 2)) * 2 + (core ^ (n % 2))
            part = jnp.dot(
                piece[...], ref[pl.ds(pl.multiple_of(block * 128, 128), 128), :], preferred_element_type=F32
            )
            total = part if total is None else total + part
        pair, next_ = total[:2 * cols], total[2 * cols:]
        return jnp.concatenate([jnp.where(even, next_, pair), jnp.where(even, pair, next_)], 0)

    fill(over_all, (2, 3, 4, 5))
    fill(over_pieces, (0, 1, 6, 7))
    zeros = jnp.zeros((cols, 128), F32)
    pair = pair_ref[pl.ds(2 * cols, 2 * cols), :].astype(F32)
    next_ = next_ref[pl.ds(0, 2 * cols), :].astype(F32)
    cotf[pl.ds(0, 2 * cols), :] = jnp.where(even, next_, pair)
    cotf[pl.ds(2 * cols, 8 * cols), :] = cot_ref[...].astype(F32)
    cotf[pl.ds(10 * cols, 2 * cols), :] = jnp.where(even, pair, next_)
    for i in range(2):
        cots[i, pl.ds(0, cols, stride=8), :] = zeros
        cots[i, pl.ds(7, cols, stride=8), :] = zeros
        for k in range(6):
            cots[i, pl.ds(k + 1, cols, stride=8), :] = cotf[pl.ds(2 * cols * k + i, cols, stride=2), :]

    group = TAPS * 8
    for end in (0, cols + 1):
        rows[pl.ds(end * group, group), :] = jnp.zeros((group, 256), BF)
        gp[pl.ds(end * 64, 64), :] = jnp.zeros((64, 256), BF)

    def spread(l, _):
        at = l * 8
        taps = []
        for i in range(4):
            v = cs[i, pl.ds(at, 8), :]
            taps.append((shift_lanes(v, 1), v, shift_lanes(v, -1)))
        for i in range(2):
            block = [taps[i + a][b] for a in range(3) for b in range(3)]
            block.append(jnp.zeros((8, 128), F32))
            rows[pl.ds((l + 1) * group, group), pl.ds(i * 128, 128)] = jnp.concatenate(block, 0).astype(BF)
        return 0


    for copy in fetched:
        copy.wait()
    wf = wf_ref[...]
    wb = wb_ref[...]

    def forward(l, _):
        kind = 0 if l == 0 else 2 if l == cols - 1 else 1
        window = rows[pl.ds(l * group, 3 * group), :]
        u = jnp.dot(wf, window, preferred_element_type=F32)
        b = bias_ref[pl.ds(kind * 64, 64), :]
        u = u + jnp.concatenate([b, b], 1)
        th = jnp.tanh(u)
        q = u * th
        g = (1.0 + u) + th * (1.0 - q)
        s = u + q
        at = l * 8
        cot = jnp.concatenate([cots[0, pl.ds(at, 8), :], cots[1, pl.ds(at, 8), :]], 1)
        total = jnp.zeros((8, 256), F32)
        out = []
        for o in range(8):
            w = bias_ref[pl.ds(192 + o * 8, 8), :]
            w = jnp.concatenate([w, w], 1)
            total = total + w * s[o * 8:o * 8 + 8]
            out.append(g[o * 8:o * 8 + 8] * (cot * (0.5 * w)))
        gp[pl.ds((l + 1) * 64, 64), :] = jnp.concatenate(out, 0).astype(BF)
        sc[0, pl.ds(at, 8), :] = total[:, :128]
        sc[1, pl.ds(at, 8), :] = total[:, 128:]
        return 0


    def backward(m, _):
        window = gp[pl.ds(m * 128, 256), :]
        t = jnp.dot(wb, window, preferred_element_type=F32)
        at = m * 8
        for io in range(4):
            part = []
            for b in range(3):
                pieces = []
                for a in range(3):
                    i = io - a
                    if 0 <= i < 2:
                        pieces.append(t[(b * 3 + a) * 8:(b * 3 + a) * 8 + 8, i * 128:(i + 1) * 128])
                part.append(functools.reduce(jnp.add, pieces))
            gs[io, pl.ds(at, 8), :] = shift_lanes(part[0], -1) + part[1] + shift_lanes(part[2], 1)
        return 0

    lag = 8
    for l in range(cols + 2 * lag):
        if l < cols:
            spread(l, 0)
        if lag <= l < cols + lag:
            forward(l - lag, 0)
        if l >= 2 * lag and l % 2 == 1:
            backward((l - 2 * lag) // 2, 0)

    for k in range(4):
        for i in range(2):
            cotf[pl.ds(2 * cols * k + i, cols, stride=2), :] = sc[i, pl.ds(k + 2, cols, stride=8), :]
    score_ref[...] = cotf[pl.ds(0, 8 * cols), :].astype(BF)
    for k in range(4):
        here = pl.ds(k * cols, cols)
        lo, mid_lo, mid_hi, hi = (gs[i, pl.ds(k, cols, stride=4), :] for i in range(4))
        g_ref[here, pl.ds(0, 128)] = mid_lo
        g_ref[here, pl.ds(128, 128)] = mid_hi
        far_out[here, :] = jnp.where(first, lo, hi).astype(BF)
        near_out[here, :] = jnp.where(first, hi, lo).astype(BF)


def conv(cols, scale, spot, weights, tgt, src, far, near, pair, next_, cot, halos):
    vmem = pl.BlockSpec(memory_space=pltpu.VMEM)
    smem = pl.BlockSpec(memory_space=pltpu.SMEM)
    n = 4 * cols
    return pl.pallas_call(
        functools.partial(conv_kernel, cols, scale),
        out_shape=(
            jax.ShapeDtypeStruct((8 * cols, 128), BF),
            jax.ShapeDtypeStruct((n, 256), F32),
            jax.ShapeDtypeStruct((n, 128), BF),
            jax.ShapeDtypeStruct((n, 128), BF),
        ),
        in_specs=[smem] + [pl.BlockSpec(memory_space=pltpu.HBM)] * 3 + [vmem] * (7 + len(halos)),
        out_specs=(vmem,) * 4,
        scratch_shapes=[
            pltpu.VMEM((4, 8 * cols, 128), F32),
            pltpu.VMEM(((cols + 2) * TAPS * 8, 256), BF),
            pltpu.VMEM((12 * cols, 128), F32),
            pltpu.VMEM((2, 8 * cols, 128), F32),
            pltpu.VMEM(((cols + 2) * 64, 256), BF),
            pltpu.VMEM((2, 8 * cols, 128), F32),
            pltpu.VMEM((4, 4 * cols, 128), F32),
            *(pltpu.VMEM(w.shape, w.dtype) for w in weights),
            pltpu.SemaphoreType.DMA((3,)),
        ],
        compiler_params=pltpu.CompilerParams(vmem_limit_bytes=40 * 2**20),
        cost_estimate=pl.CostEstimate(flops=4 * 10**9, transcendentals=10**7, bytes_accessed=4 * 10**6),
    )(spot, *weights, tgt, src, far, near, pair, next_, cot, *halos)


def tables():
    spread = np.zeros((9, 8, 256), np.float32)
    mask = np.zeros((9, 8, 256), np.float32)
    place = np.zeros((9, 8, 8, 256), np.float32)
    for d in range(3):
        for e in range(3):
            for m in range(1, 7):
                for x in range(9):
                    lane = (e * TAPS + x) * 8 + m + d - 1
                    spread[x, m, (e * TAPS + x) * 8:(e * TAPS + x) * 8 + 8] = 1
                    mask[d * 3 + e, m, lane] = 1
            for s in range(2):
                for k in range(4):
                    for o in range(8):
                        place[d * 3 + e, o, s * 4 + k, (s + 2 - e) * 64 + o * 8 + k + 3 - d] = 1
    return (
        jnp.asarray(spread.reshape(3, 3, 2048), BF),
        jnp.asarray(mask.reshape(9, 1, 2048), F32),
        jnp.asarray(place.reshape(9, 8, 2048), BF),
    )


def filters_kernel(
    total_rows,
    row_ref, wt_ref, ws_ref, b_src_ref, b_tgt_ref, w_out_ref, spread_ref, mask_ref, place_ref,
    wf_ref, wb_ref, bias_ref, forward, adjoint,
):
    over_first = (((0,), (0,)), ((), ()))
    source = lanes = None
    for a in range(3):
        part = lax.dot_general(ws_ref[a], spread_ref[a], over_first, preferred_element_type=F32)
        source = part if source is None else source + part
    out = None
    for n in range(9):
        part = jnp.dot(wt_ref[n], (source * mask_ref[n]).astype(BF), preferred_element_type=F32)
        out = part if out is None else out + part
        part = lax.dot_general(wt_ref[n], place_ref[n], over_first, preferred_element_type=F32)
        lanes = part if lanes is None else lanes + part
    for m in range(8):
        for h in range(2):
            at = m * 256 + h * 128
            forward[h, pl.ds(m, 8, stride=8), :] = 0.5 * out[:, at:at + 128]
    wf_ref[...] = jnp.concatenate([forward[0], forward[1, :, :3 * TAPS * 8 - 128]], 1).astype(BF)
    lanes = lanes.astype(BF)
    for a in range(3):
        part = jnp.dot(ws_ref[a], lanes, preferred_element_type=F32)
        for c in range(8):
            for h in range(2):
                at = c * 256 + h * 128
                adjoint[h, pl.ds(a * 8 + c, 3, stride=24), :] = part[:, at:at + 128]
    wb_ref[...] = jnp.concatenate([adjoint[0], adjoint[1]], 1).astype(BF)

    def column(ref):
        v = jnp.broadcast_to(ref[...], (8, 8))
        same = lax.broadcasted_iota(jnp.int32, (8, 8), 0) == lax.broadcasted_iota(jnp.int32, (8, 8), 1)
        return jnp.sum(jnp.where(same, v, 0.0), 1, keepdims=True)

    b_tgt, w_out = column(b_tgt_ref), column(w_out_ref)
    lift = [jnp.sum(wt_ref[n].astype(F32) * b_src_ref[...], 1, keepdims=True) for n in range(9)]
    for kind in range(3):
        along = []
        for d in range(3):
            parts = [lift[d * 3 + e] for e in range(3) if (kind, e) not in ((0, 0), (2, 2))]
            along.append(functools.reduce(jnp.add, parts))
        for m in range(8):
            total = b_tgt
            for d in range(3):
                if 1 <= m <= 6:
                    row = row_ref[0] + (m + d - 3)
                    inside = jnp.logical_and(row >= 0, row < total_rows)
                    total = total + jnp.where(inside, along[d], 0.0)
            bias_ref[pl.ds(kind * 64 + m, 8, stride=8), :] = jnp.broadcast_to(0.5 * total, (8, 128))
    for m in range(8):
        bias_ref[pl.ds(192 + m, 8, stride=8), :] = jnp.broadcast_to(w_out, (8, 128))


def filters(w_src, b_src, w_tgt, b_tgt, w_out, first_row, total_rows):
    vmem = pl.BlockSpec(memory_space=pltpu.VMEM)
    smem = pl.BlockSpec(memory_space=pltpu.SMEM)
    return pl.pallas_call(
        functools.partial(filters_kernel, total_rows),
        out_shape=(
            jax.ShapeDtypeStruct((64, 3 * TAPS * 8), BF),
            jax.ShapeDtypeStruct((72, 256), BF),
            jax.ShapeDtypeStruct((256, 128), F32),
        ),
        in_specs=[smem] + [vmem] * 8,
        out_specs=(vmem,) * 3,
        scratch_shapes=[pltpu.VMEM((2, 64, 128), F32), pltpu.VMEM((2, 72, 128), F32)],
        cost_estimate=pl.CostEstimate(flops=4 * 10**9, transcendentals=0, bytes_accessed=10**6),
    )(
        first_row.astype(jnp.int32)[None],
        w_tgt.transpose(2, 3, 0, 1).reshape(9, 8, 8),
        w_src.transpose(1, 2, 0),
        b_src[None], b_tgt[None], w_out[None],
        *tables(),
    )


SRC = ("z", "core")
TGT = ("y", "x", "zh")
SIZES = {"z": 4, "core": 2, "y": 4, "x": 4, "zh": 2}


def moved(x, move):
    n_src, n_tgt = lax.axis_size(SRC), lax.axis_size(TGT)
    pairs = []
    for a in range(n_src):
        for b in range(n_tgt):
            c, d = move(a, b)
            if 0 <= c < n_src and 0 <= d < n_tgt:
                pairs.append((a * n_tgt + b, c * n_tgt + d))
    return lax.ppermute(x, SRC + TGT, pairs)


def far_row(a, b):
    return (a + 1 if a % 2 else a - 1, b)


def near_row(a, b):
    return (a ^ 1, b)


def body(src_feat, tgt_feat, w_src, b_src, w_tgt, b_tgt, w_out, cotangent):
    rows_k, cols, rows_i, cols_j = cotangent.shape
    chans = tgt_feat.shape[2]
    scale = chans ** (-0.5)
    n_src, n_tgt = lax.axis_size(SRC), lax.axis_size(TGT)
    s, t, z, core, zh = (lax.axis_index(a) for a in (SRC, TGT, "z", "core", "zh"))
    first = core == 0
    block = chans // n_tgt
    pixels = rows_i * cols_j

    tgt_flat = tgt_feat.reshape(rows_k * cols, chans)
    cot = cotangent.reshape(rows_k * cols * rows_i, cols_j)
    width = chans // n_src
    hops = n_src // 2

    piece = src_feat.reshape(pixels, block).T
    line = cols * rows_i

    def edge(last, swap):
        k = jnp.where(last, rows_k - 2, 0)
        part = lax.dynamic_slice(tgt_feat, (k, 0, s * width), (2, cols, width)).reshape(2 * cols, width)
        k = jnp.where(last, rows_k - 1, 0)
        parts = [part, lax.dynamic_slice(cot, (k * line, 0), (line, cols_j))]
        return jnp.concatenate(parts[::-1] if swap else parts, 0)

    even = zh == 0
    other = moved(piece, lambda a, b: (a, b ^ 1))
    pair_e, next_e = edge(even, False), edge(~even, True)
    next_e, other = lax.optimization_barrier((next_e, other))
    pair = moved(pair_e, lambda a, b: (a, b ^ 1))
    next_ = moved(next_e, lambda a, b: (a, b + 1 if b % 2 else b - 1))
    upper = lax.broadcasted_iota(jnp.int32, pair.shape, 0) < 2 * cols
    share = jnp.where(upper, pair, next_)
    w_src, b_src, w_tgt, b_tgt, share = lax.optimization_barrier((w_src, b_src, w_tgt, b_tgt, share))
    weights = filters(w_src, b_src, w_tgt, b_tgt, w_out, t * rows_k, rows_k * n_tgt)
    shares = [share]
    for m in range(1, hops):
        shares.append(moved(share, lambda a, b, m=m: (a ^ (2 * m), b)))
    share, late = lax.optimization_barrier((share, tgt_flat))
    tgt_t = lax.optimization_barrier(late.T)

    both = jnp.where(even, jnp.concatenate([piece, other], 0), jnp.concatenate([other, piece], 0))
    plane = n_tgt // 2
    src_t = lax.all_to_all(
        jnp.broadcast_to(both[None], (plane, 2 * block, pixels)), ("y", "x"), 0, 0, tiled=True
    ).reshape(chans, pixels)
    src_t, shares[1], shares[2], *weights = lax.optimization_barrier((src_t, shares[1], shares[2], *weights))
    halos = []
    for mine in shares:
        halos += [mine, moved(mine, near_row)]
    low, high = src_t[:, :cols_j], src_t[:, cols_j:]
    near = moved(jnp.where(first, high, low), near_row)
    far = moved(jnp.where(first, low, high), far_row)

    spot = jnp.stack([z, core, zh]).astype(jnp.int32)
    score, g_own, to_far, to_near = conv(
        cols, scale, spot, weights, tgt_flat, src_t, far, near, pair, next_, cot, halos
    )
    from_near = moved(to_near, near_row)
    from_far = moved(to_far, far_row)
    g = jnp.concatenate(
        [
            g_own[:, :cols_j] + jnp.where(first, from_far, from_near).astype(F32),
            g_own[:, cols_j:] + jnp.where(first, from_near, from_far).astype(F32),
        ],
        1,
    ).astype(BF)

    cut = src_t.reshape(n_src, width, pixels)

    def blocks(side):
        return jnp.concatenate(
            [lax.dynamic_index_in_dim(cut, (z ^ m) * 2 + side, 0, False) for m in range(hops)], 0
        )

    over = (((1,), (1,)), ((), ()))
    other = lax.dot_general(g, blocks(1 - core), over, preferred_element_type=F32) * scale
    got = moved(other.astype(BF), near_row)
    mine = lax.dot_general(g, blocks(core), over, preferred_element_type=F32) * scale
    both = mine + got.astype(F32)
    total = both[:, :width]
    for m in range(1, hops):
        total = total + moved(
            both[:, m * width:(m + 1) * width].astype(BF), lambda a, b, m=m: (a ^ (2 * m), b)
        ).astype(F32)
    grad_tgt = total.reshape(rows_k, cols, width)

    part = jnp.dot(tgt_t, g, preferred_element_type=F32) * scale
    parts = lax.all_to_all(
        part.astype(BF).reshape(plane, 2 * block, pixels), ("y", "x"), 0, 0, tiled=True
    )
    halves = jnp.sum(parts.astype(F32), 0).reshape(2, block, pixels)
    keep = lax.dynamic_index_in_dim(halves, zh, 0, False)
    send = lax.dynamic_index_in_dim(halves, 1 - zh, 0, False)
    grad_src = keep + moved(send.astype(BF), lambda a, b: (a, b ^ 1)).astype(F32)
    return (score.reshape(cotangent.shape), grad_src.reshape(block, rows_i, cols_j), grad_tgt)


def solution(mesh):
    fine = jax.sharding.Mesh(mesh.devices.reshape(tuple(SIZES.values())), tuple(SIZES))
    placed = (
        P(SRC, None, TGT),
        P(TGT, None, None),
        P(),
        P(),
        P(),
        P(),
        P(),
        P(TGT, None, SRC, None),
    )
    return jax.shard_map(
        body,
        mesh=fine,
        in_specs=placed,
        out_specs=(P(TGT, None, SRC, None), P(TGT, SRC, None), P(TGT, None, SRC)),
        check_vma=False,
    )
```
